32 devices in a mesh: dp: 8 (over y, x, core), tensor: 4 (over z).
Axes of the slice: x: 2, y: 2, z: 4, core: 2. Of those that a mesh axis runs over, the one named last changes fastest.
Arguments:
- tokens_in: bfloat16 [32, 577, 1024], P('dp'), may hold values from -6 to 6
- norm1_gain: float32 [1024], replicated, may hold values from 0.5 to 1.5
- norm1_bias: float32 [1024], replicated, may hold values from -3 to 3
- w_qkv: bfloat16 [1024, 3, 16, 64], P(None, None, 'tensor'), may hold values from -0.1875 to 0.1875
- bias_qv: float32 [2, 16, 64], P(None, 'tensor'), may hold values from -3 to 3
- w_out: bfloat16 [16, 64, 1024], P('tensor'), may hold values from -0.75 to 0.75
- bias_out: float32 [1024], replicated, may hold values from -3 to 3
- norm2_gain: float32 [1024], replicated, may hold values from 0.5 to 1.5
- norm2_bias: float32 [1024], replicated, may hold values from -3 to 3
- w_up: bfloat16 [1024, 4096], P(None, 'tensor'), may hold values from -0.1875 to 0.1875
- bias_up: float32 [4096], P('tensor'), may hold values from -3 to 3
- w_down: bfloat16 [4096, 1024], P('tensor'), may hold values from -0.09375 to 0.09375
- bias_down: float32 [1024], replicated, may hold values from -3 to 3
- cotangent: bfloat16 [32, 577, 1024], P('dp'), may hold values from -6 to 6
Outputs:
- block_out: bfloat16 [32, 577, 1024], P('dp')
- grad_input: float32 [32, 577, 1024], P('dp')
- grad_norm1_gain: float32 [1024], replicated
- grad_norm1_bias: float32 [1024], replicated
- grad_w_qkv: float32 [1024, 3, 16, 64], P(None, None, 'tensor')
- grad_bias_qv: float32 [2, 16, 64], P(None, 'tensor')
- grad_w_out: float32 [16, 64, 1024], P('tensor')
- grad_bias_out: float32 [1024], replicated
- grad_norm2_gain: float32 [1024], replicated
- grad_norm2_bias: float32 [1024], replicated
- grad_w_up: float32 [1024, 4096], P(None, 'tensor')
- grad_bias_up: float32 [4096], P('tensor')
- grad_w_down: float32 [4096, 1024], P('tensor')
- grad_bias_down: float32 [1024], replicated
The draws below stay inside these ranges and needn't reach their ends.
All inputs are finite; a program needn't handle non-finite values.
Results may differ from the reference program's by a relative error of at most 0.024.
Values may be sent and summed in bfloat16 or wider, within the bound.
No kernel may reach another device: no remote copies, remote signals or barrier semaphores. Data moves between devices by JAX's collectives and lax.ppermute only.
A program may use at most 256 MiB of HBM per device.

```python
import jax
import jax.numpy as jnp
from jax import lax

D = 1024
HEADS = 16
DH = 64
FF = 4096
S = 577
IMG_DEV = 4
IMAGES = 32
N_TENSOR = 4


def draw_tokens_in(key, part):
    values = jnp.clip(jax.random.normal(jax.random.fold_in(key, 21), (IMAGES, S, D), jnp.float32), -6.0, 6.0)
    return values.astype(jnp.bfloat16)


def draw_w_qkv(key, part):
    scale = D ** (-0.5)
    values = jnp.clip(jax.random.normal(jax.random.fold_in(key, 32), (D, 3, HEADS, DH), jnp.float32), -5.5, 5.5) * scale
    return values.astype(jnp.bfloat16)


def level_of(key, dims, cuts, low, largest):
    factor_of = 1.0
    for position, blocks in cuts:
        heights = jax.random.uniform(jax.random.fold_in(jax.random.fold_in(key, 6), position), (blocks,), jnp.float32, low / len(cuts), largest / len(cuts))
        factor_of = factor_of * jnp.repeat(jnp.exp(heights), dims[position] // blocks).reshape((-1,) + (1,) * (len(dims) - 1 - position))
    return factor_of


def scatter_about(stream_key, shape, width, bound, cuts=(), held_as=jnp.bfloat16):
    values = jax.random.normal(stream_key, shape, jnp.float32) * width
    if len(cuts) > 0:
        values = level_of(stream_key, shape, cuts, -0.22, 0.18) * values
    return jnp.clip(values, min=-bound, max=bound).astype(held_as)


def setup_inputs(seed: int = 0) -> dict:
    key_of = jax.random.split(jax.random.key(seed), 15)
    tokens_in = draw_tokens_in(jax.random.fold_in(key_of[14], 71), 0)
    norm1_gain = jnp.clip(1.0 + 0.1 * jax.random.normal(key_of[1], (D,), jnp.float32), 0.5, 1.5)
    norm1_bias = scatter_about(key_of[2], (D,), 0.5, 3.0, (), jnp.float32)
    w_qkv = draw_w_qkv(jax.random.fold_in(key_of[14], 71), 0)
    bias_qv = scatter_about(key_of[4], (2, HEADS, DH), 0.5, 3.0, ((1, 4),), jnp.float32)
    w_out = scatter_about(key_of[5], (HEADS, DH, D), (D // 16) ** -0.5, 0.75, ((0, 4),))
    bias_out = scatter_about(key_of[6], (D,), 0.5, 3.0, (), jnp.float32)
    norm2_gain = jnp.clip(1.0 + 0.1 * jax.random.normal(key_of[7], (D,), jnp.float32), 0.5, 1.5)
    norm2_bias = scatter_about(key_of[8], (D,), 0.5, 3.0, (), jnp.float32)
    w_up = scatter_about(key_of[9], (D, FF), D ** -0.5, 0.1875, ((1, 4),))
    bias_up = scatter_about(key_of[10], (FF,), 0.5, 3.0, ((0, 4),), jnp.float32)
    w_down = scatter_about(key_of[11], (FF, D), FF ** -0.5, 0.09375, ((0, 4),))
    bias_down = scatter_about(key_of[12], (D,), 0.5, 3.0, (), jnp.float32)
    cotangent = scatter_about(key_of[13], (IMAGES, S, D), 1.0, 6.0, ((0, 8),))
    return dict(tokens_in=tokens_in, norm1_gain=norm1_gain, norm1_bias=norm1_bias, w_qkv=w_qkv, bias_qv=bias_qv, w_out=w_out, bias_out=bias_out, norm2_gain=norm2_gain, norm2_bias=norm2_bias, w_up=w_up, bias_up=bias_up, w_down=w_down, bias_down=bias_down, cotangent=cotangent)


inv_root2 = 0.7071067811865476
inv_root_2pi = 0.3989422804014327

def to_bf(value):
    return lax.optimization_barrier(value.astype(jnp.bfloat16))

def rounded(value):
    return lax.optimization_barrier(value.astype(jnp.bfloat16)).astype(jnp.float32)

def layer_norm(values, gain, shift):
    centre = lax.optimization_barrier(jnp.mean(values, axis=-1, keepdims=True))
    centred = values - centre
    spread = lax.optimization_barrier(jnp.mean(centred * centred, axis=-1, keepdims=True))
    inv_std = lax.rsqrt(spread + 1e-06)
    whitened = centred * inv_std
    return (whitened, inv_std, whitened * gain + shift)

def norm_back(grad_out, whitened, inv_std, gain):
    grad_white = grad_out * gain
    inner_part = grad_white - lax.optimization_barrier(jnp.mean(grad_white, axis=-1, keepdims=True)) - whitened * lax.optimization_barrier(jnp.mean(grad_white * whitened, axis=-1, keepdims=True))
    return (inv_std * inner_part, lax.optimization_barrier(jnp.sum(grad_out * whitened, axis=0)), lax.optimization_barrier(jnp.sum(grad_out, axis=0)))

def gelu(pre_act):
    return 0.5 * pre_act * (1.0 + lax.erf(pre_act * inv_root2))

def gelu_slope(pre_act):
    return 0.5 * (1.0 + lax.erf(pre_act * inv_root2)) + pre_act * inv_root_2pi * jnp.exp(-0.5 * pre_act * pre_act)

def attend(queries, key_rows, values, score_scale):
    scores = jnp.einsum('qhd,khd->hqk', queries.astype(jnp.float32), key_rows.astype(jnp.float32)) * score_scale
    row_max = lax.optimization_barrier(jnp.max(scores, axis=-1, keepdims=True))
    expos = jnp.exp(scores - row_max)
    expsum = lax.optimization_barrier(jnp.sum(expos, axis=-1, keepdims=True))
    probs = rounded(expos / expsum)
    attended = to_bf(jnp.einsum('hqk,khd->qhd', probs, values.astype(jnp.float32)))
    return (attended, (row_max + jnp.log(expsum))[..., 0])

def attend_back(queries, key_rows, values, upstream, log_norm, score_scale):
    scores = jnp.einsum('qhd,khd->hqk', queries.astype(jnp.float32), key_rows.astype(jnp.float32)) * score_scale
    probs = jnp.exp(scores - log_norm[..., None])
    up_float = upstream.astype(jnp.float32)
    grad_values = jnp.einsum('hqk,qhd->khd', rounded(probs), up_float)
    grad_prob = jnp.einsum('qhd,khd->hqk', up_float, values.astype(jnp.float32))
    row_delta = lax.optimization_barrier(jnp.sum(probs * grad_prob, axis=-1, keepdims=True))
    grad_score = rounded(probs * (grad_prob - row_delta) * score_scale)
    grad_queries = jnp.einsum('hqk,khd->qhd', grad_score, key_rows.astype(jnp.float32))
    grad_keys = jnp.einsum('hqk,qhd->khd', grad_score, queries.astype(jnp.float32))
    return (grad_queries, grad_keys, grad_values)

def block_pass(tokens_blk, cot_blk, params):
    norm1_gain, norm1_bias, w_qkv, bias_qv, w_out, bias_out, norm2_gain, norm2_bias, w_up, bias_up, w_down, bias_down = params
    image_count = tokens_blk.shape[0]
    tok_rows = image_count * S
    groups = N_TENSOR
    head_group = HEADS // groups
    hidden_group = FF // groups
    score_scale = DH ** (-0.5)
    image_shape = (image_count, S, HEADS, DH)
    x_float = tokens_blk.reshape(tok_rows, D).astype(jnp.float32)
    white1, inv1, normed1 = layer_norm(x_float, norm1_gain, norm1_bias)
    first_in = to_bf(normed1)
    projected = jnp.dot(first_in, w_qkv.reshape(D, 3 * HEADS * DH), preferred_element_type=jnp.float32).reshape(tok_rows, 3, HEADS, DH)
    queries = to_bf(projected[:, 0] + bias_qv[0]).reshape(image_shape)
    key_rows = to_bf(projected[:, 1]).reshape(image_shape)
    values = to_bf(projected[:, 2] + bias_qv[1]).reshape(image_shape)
    attended, log_norm = lax.map(lambda packed: attend(packed[0], packed[1], packed[2], score_scale), (queries, key_rows, values))
    head_flat = attended.reshape(tok_rows, HEADS * DH)
    partials = jnp.einsum('rgk,gke->rge', head_flat.reshape(tok_rows, groups, head_group * DH).astype(jnp.float32), w_out.reshape(groups, head_group * DH, D).astype(jnp.float32))
    hidden1 = x_float + lax.optimization_barrier(jnp.sum(rounded(partials), axis=1)) + bias_out
    white2, inv2, normed2 = layer_norm(hidden1, norm2_gain, norm2_bias)
    second_in = to_bf(normed2)
    pre_act = jnp.dot(second_in, w_up, preferred_element_type=jnp.float32) + bias_up
    hidden_act = to_bf(gelu(pre_act))
    partials = jnp.einsum('rgk,gke->rge', hidden_act.reshape(tok_rows, groups, hidden_group).astype(jnp.float32), w_down.reshape(groups, hidden_group, D).astype(jnp.float32))
    result = hidden1 + lax.optimization_barrier(jnp.sum(rounded(partials), axis=1)) + bias_down
    block_out = result.astype(jnp.bfloat16)
    grad_out = cot_blk.reshape(tok_rows, D)
    grad_float = grad_out.astype(jnp.float32)
    grad_bias_down = lax.optimization_barrier(jnp.sum(grad_float, axis=0))
    grad_w_down = jnp.dot(hidden_act.T, grad_out, preferred_element_type=jnp.float32)
    grad_hidden = jnp.dot(grad_out, w_down.T, preferred_element_type=jnp.float32)
    grad_pre = grad_hidden * gelu_slope(pre_act)
    grad_bias_up = lax.optimization_barrier(jnp.sum(grad_pre, axis=0))
    grad_pre_bf = to_bf(grad_pre)
    grad_w_up = jnp.dot(second_in.T, grad_pre_bf, preferred_element_type=jnp.float32)
    partials = jnp.einsum('rgk,egk->rge', grad_pre_bf.reshape(tok_rows, groups, hidden_group).astype(jnp.float32), w_up.reshape(D, groups, hidden_group).astype(jnp.float32))
    grad_norm2_in, grad_norm2_gain, grad_norm2_bias = norm_back(lax.optimization_barrier(jnp.sum(rounded(partials), axis=1)), white2, inv2, norm2_gain)
    grad_hidden1 = grad_float + grad_norm2_in
    grad_bias_out = lax.optimization_barrier(jnp.sum(grad_hidden1, axis=0))
    grad_h1_bf = to_bf(grad_hidden1)
    grad_w_out = jnp.dot(head_flat.T, grad_h1_bf, preferred_element_type=jnp.float32).reshape(HEADS, DH, D)
    upstream = to_bf(jnp.dot(grad_h1_bf, w_out.reshape(HEADS * DH, D).T, preferred_element_type=jnp.float32))
    grad_queries, grad_keys, grad_values = lax.map(lambda packed: attend_back(packed[0], packed[1], packed[2], packed[3], packed[4], score_scale), (queries, key_rows, values, upstream.reshape(image_shape), log_norm))
    grad_queries = grad_queries.reshape(tok_rows, HEADS, DH)
    grad_keys = grad_keys.reshape(tok_rows, HEADS, DH)
    grad_values = grad_values.reshape(tok_rows, HEADS, DH)
    grad_bias_qv = jnp.stack([lax.optimization_barrier(jnp.sum(grad_queries, axis=0)), lax.optimization_barrier(jnp.sum(grad_values, axis=0))])
    grad_qkv = to_bf(jnp.stack([grad_queries, grad_keys, grad_values], axis=1))
    grad_w_qkv = jnp.dot(first_in.T, grad_qkv.reshape(tok_rows, 3 * HEADS * DH), preferred_element_type=jnp.float32).reshape(D, 3, HEADS, DH)
    partials = jnp.einsum('rcgk,ecgk->rge', grad_qkv.reshape(tok_rows, 3, groups, head_group * DH).astype(jnp.float32), w_qkv.reshape(D, 3, groups, head_group * DH).astype(jnp.float32))
    grad_norm1_in, grad_norm1_gain, grad_norm1_bias = norm_back(lax.optimization_barrier(jnp.sum(rounded(partials), axis=1)), white1, inv1, norm1_gain)
    grad_input = grad_hidden1 + grad_norm1_in
    grads = (grad_norm1_gain, grad_norm1_bias, grad_w_qkv, grad_bias_qv, grad_w_out, grad_bias_out, grad_norm2_gain, grad_norm2_bias, grad_w_up, grad_bias_up, grad_w_down, grad_bias_down)
    return (block_out.reshape(image_count, S, D), grad_input.reshape(image_count, S, D), grads)

def reference(tokens_in, norm1_gain, norm1_bias, w_qkv, bias_qv, w_out, bias_out, norm2_gain, norm2_bias, w_up, bias_up, w_down, bias_down, cotangent):
    params = (norm1_gain, norm1_bias, w_qkv, bias_qv, w_out, bias_out, norm2_gain, norm2_bias, w_up, bias_up, w_down, bias_down)
    blocks = IMAGES // IMG_DEV
    zeros = tuple((jnp.zeros(param.shape, jnp.float32) for param in params))

    def step(carry, item):
        out_blk, grad_blk, grads = block_pass(item[0], item[1], params)
        return (tuple((left + right for left, right in zip(carry, grads))), (out_blk, grad_blk))
    totals, (outputs, grad_inputs) = lax.scan(step, zeros, (tokens_in.reshape(blocks, IMG_DEV, S, D), cotangent.reshape(blocks, IMG_DEV, S, D)))
    return (outputs.reshape(IMAGES, S, D), grad_inputs.reshape(IMAGES, S, D), totals[0], totals[1], totals[2], totals[3], totals[4], totals[5], totals[6], totals[7], totals[8], totals[9], totals[10], totals[11])
```

```python
import functools

import jax
import jax.numpy as jnp
from jax import lax
from jax.experimental import pallas as pl
from jax.experimental.pallas import tpu as pltpu
from jax.sharding import PartitionSpec as P

F32 = jnp.float32
BF16 = jnp.bfloat16
EPS = 1e-06
INV_ROOT2 = 0.7071067811865476
INV_ROOT_2PI = 0.3989422804014327
LOG2E = 1.4426950408889634
VMEM_BYTES = 60 * 1024 * 1024


def mm(a, b):
    return lax.dot_general(a, b, (((1,), (0,)), ((), ())), preferred_element_type=F32)


def mm_nt(a, b):
    return lax.dot_general(a, b, (((1,), (1,)), ((), ())), preferred_element_type=F32)


def mm_tn(a, b):
    return lax.dot_general(a, b, (((0,), (0,)), ((), ())), preferred_element_type=F32)


def whiten(values):
    centred = values - jnp.mean(values, axis=-1, keepdims=True)
    inv_std = lax.rsqrt(jnp.mean(centred * centred, axis=-1, keepdims=True) + EPS)
    return centred * inv_std, inv_std


def norm_back(grad_out, white, inv_std, gain):
    grad_white = grad_out * gain
    inner = (
        grad_white
        - jnp.mean(grad_white, axis=-1, keepdims=True)
        - white * jnp.mean(grad_white * white, axis=-1, keepdims=True)
    )
    return inv_std * inner


def row_sum(values):
    return jnp.sum(values, axis=0, keepdims=True)


def joined(ref):
    block = ref[...]
    return block.reshape(block.shape[0] * block.shape[2], block.shape[3])


def put(ref, value):
    ref[...] = value.reshape(ref.shape).astype(ref.dtype)


def fwd_kernel(
    heads, head_size, tokens, x_ref, g1_ref, b1_ref, wqkv_ref, bqkv_ref, wout_ref, bout_ref,
    g2_ref, b2_ref, u1_ref, qkv_ref, o_ref, h1_ref, u2_ref, acc_ref,
):
    step = pl.program_id(0)

    @pl.when(step == 0)
    def _():
        white, _ = whiten(x_ref[...].astype(F32))
        u1_ref[...] = (white * g1_ref[...] + b1_ref[...]).astype(BF16)
        acc_ref[...] = jnp.zeros_like(acc_ref)

    qkv = (mm_nt(u1_ref[...], joined(wqkv_ref)) + bqkv_ref[0]).astype(BF16)
    qkv_ref[...] = qkv
    inner = heads * head_size
    rows = qkv.shape[0]
    factor = LOG2E * head_size ** (-0.5)
    real = lax.broadcasted_iota(jnp.int32, (1, rows), 1) < tokens
    outs = []
    for head in range(heads):
        q = qkv[:, head * head_size : (head + 1) * head_size]
        k = qkv[:, inner + head * head_size : inner + (head + 1) * head_size]
        v = qkv[:, 2 * inner + head * head_size : 2 * inner + (head + 1) * head_size]
        scores = jnp.where(real, mm_nt(q, k) * factor, -1e30)
        expos = jnp.exp2(scores - jnp.max(scores, axis=-1, keepdims=True))
        total = jnp.sum(expos, axis=-1, keepdims=True)
        outs.append((mm(expos.astype(BF16), v) / total).astype(BF16))
    o = jnp.concatenate(outs, axis=1)
    o_ref[...] = o
    acc_ref[...] += mm(o, joined(wout_ref))

    @pl.when(step == pl.num_programs(0) - 1)
    def _():
        hidden1 = x_ref[...].astype(F32) + acc_ref[...] + bout_ref[...]
        h1_ref[...] = hidden1
        white, _ = whiten(hidden1)
        u2_ref[...] = (white * g2_ref[...] + b2_ref[...]).astype(BF16)


def mlp_kernel(
    u2_ref, h1_ref, c_ref, wup_ref, bup_ref, wdn_ref, bdn_ref, g2_ref,
    out_ref, dh1_ref, gwup_ref, gwdn_ref, gbup_ref, small_ref, acc_ref, dacc_ref,
):
    step = pl.program_id(0) * pl.num_programs(1) + pl.program_id(1)

    @pl.when(step == 0)
    def _():
        acc_ref[...] = jnp.zeros_like(acc_ref)
        dacc_ref[...] = jnp.zeros_like(dacc_ref)

    u2 = u2_ref[...]
    c = c_ref[...]
    wup = joined(wup_ref)
    wdn = joined(wdn_ref)
    pre = mm(u2, wup) + bup_ref[0]
    half = 0.5 * (1.0 + lax.erf(pre * INV_ROOT2))
    hid = (pre * half).astype(BF16)
    slope = half + pre * INV_ROOT_2PI * jnp.exp(-0.5 * pre * pre)
    acc_ref[...] += mm(hid, wdn)
    put(gwdn_ref, mm_tn(hid, c))
    dpre = mm_nt(c, wdn) * slope
    gbup_ref[0] = row_sum(dpre)
    dpre_bf = dpre.astype(BF16)
    put(gwup_ref, mm_tn(u2, dpre_bf))
    dacc_ref[...] += mm_nt(dpre_bf, wup)

    @pl.when(step == pl.num_programs(0) * pl.num_programs(1) - 1)
    def _():
        hidden1 = h1_ref[...]
        out_ref[...] = (hidden1 + acc_ref[...] + bdn_ref[...]).astype(BF16)
        white, inv_std = whiten(hidden1)
        du2 = dacc_ref[...]
        cf = c.astype(F32)
        dh1 = cf + norm_back(du2, white, inv_std, g2_ref[...])
        dh1_ref[...] = dh1
        small_ref[...] = jnp.concatenate(
            [row_sum(cf), row_sum(du2 * white), row_sum(du2), row_sum(dh1)], axis=0
        )


def bwd_kernel(
    heads, head_size, tokens, x_ref, g1_ref, u1_ref, qkv_ref, o_ref, dh1_ref, wqkv_ref, wout_ref,
    gin_ref, gwqkv_ref, gwout_ref, gbias_ref, small_ref, dhb_ref, acc_ref, dqkv_ref,
):
    step = pl.program_id(0)

    @pl.when(step == 0)
    def _():
        dhb_ref[...] = dh1_ref[...].astype(BF16)
        acc_ref[...] = jnp.zeros_like(acc_ref)

    dhb = dhb_ref[...]
    qkv = qkv_ref[...]
    up = mm_nt(dhb, joined(wout_ref)).astype(BF16)
    put(gwout_ref, mm_tn(o_ref[...], dhb))
    inner = heads * head_size
    rows = qkv.shape[0]
    scale = head_size ** (-0.5)
    real = lax.broadcasted_iota(jnp.int32, (rows, 1), 0) < tokens
    for head in range(heads):
        q = qkv[:, head * head_size : (head + 1) * head_size]
        k = qkv[:, inner + head * head_size : inner + (head + 1) * head_size]
        v = qkv[:, 2 * inner + head * head_size : 2 * inner + (head + 1) * head_size]
        do = up[:, head * head_size : (head + 1) * head_size]
        scores = jnp.where(real, mm_nt(k, q) * (LOG2E * scale), -1e30)
        expos = jnp.exp2(scores - jnp.max(scores, axis=0, keepdims=True))
        probs = expos * (1.0 / jnp.sum(expos, axis=0, keepdims=True))
        dv = mm(probs.astype(BF16), do)
        dprob = mm_nt(v, do)
        delta = jnp.sum(probs * dprob, axis=0, keepdims=True)
        dscore = (probs * (dprob - delta) * scale).astype(BF16)
        dk = mm(dscore, q)
        dq = mm_tn(dscore, k)
        dqkv_ref[:, head * head_size : (head + 1) * head_size] = dq
        dqkv_ref[:, inner + head * head_size : inner + (head + 1) * head_size] = dk
        dqkv_ref[:, 2 * inner + head * head_size : 2 * inner + (head + 1) * head_size] = dv
    dqkv = dqkv_ref[...]
    gbias_ref[0] = row_sum(dqkv)
    dqkv_bf = dqkv.astype(BF16)
    put(gwqkv_ref, mm_tn(dqkv_bf, u1_ref[...]))
    acc_ref[...] += mm(dqkv_bf, joined(wqkv_ref))

    @pl.when(step == pl.num_programs(0) - 1)
    def _():
        white, inv_std = whiten(x_ref[...].astype(F32))
        du1 = acc_ref[...]
        gin_ref[...] = (dh1_ref[...] + norm_back(du1, white, inv_std, g1_ref[...])).astype(BF16)
        small_ref[...] = jnp.concatenate([row_sum(du1 * white), row_sum(du1)], axis=0)


def whole(shape):
    return pl.BlockSpec(shape, lambda *_: (0,) * len(shape))


def slot_block(array_shape):
    return pl.BlockSpec(
        (array_shape[0], 1, array_shape[2], array_shape[3]), lambda g, *_: (0, g, 0, 0)
    )


def call(kernel, grid, in_specs, out_specs, out_shape, scratch, name):
    return pl.pallas_call(
        kernel,
        grid=grid,
        in_specs=in_specs,
        out_specs=out_specs,
        out_shape=out_shape,
        scratch_shapes=scratch,
        compiler_params=pltpu.CompilerParams(
            dimension_semantics=("arbitrary",) * len(grid), vmem_limit_bytes=VMEM_BYTES
        ),
        name=name,
    )


class Ring:
    def __init__(self, n_dp, n_tensor):
        self.n_dp = n_dp
        self.n_tensor = n_tensor
        self.n_bits = n_dp.bit_length() - 1
        assert 1 << self.n_bits == n_dp
        self.dp_at = lax.axis_index("dp")
        self.tensor_at = lax.axis_index("tensor")

    def turn(self, value, by):
        pairs = [(i, (i + by) % self.n_tensor) for i in range(self.n_tensor)]
        return lax.ppermute(value, "tensor", pairs)

    def partner(self, value, bit):
        return lax.ppermute(value, "dp", [(i, i ^ (1 << bit)) for i in range(self.n_dp)])

    def bit_of(self, bit):
        return (self.dp_at >> bit) & 1

    def orders(self, flip):
        outer = list(range(1, self.n_bits))
        return (outer[::-1] if flip else outer) + [0] if self.n_bits else []

    def round_tensor(self, value):
        held = [value]
        for _ in range(self.n_tensor - 1):
            held.append(self.turn(held[-1], 1))
        return held

    def double(self, value, flip):
        gathered = []
        for bit in self.orders(flip):
            other = self.partner(value, bit)
            first = self.bit_of(bit) == 0
            axis = sum(1 for b in gathered if b > bit)
            value = jnp.stack(
                [jnp.where(first, value, other), jnp.where(first, other, value)], axis=axis
            )
            gathered.append(bit)
        return value

    def gather_weight(self, shard, flip):
        rows = shard.shape[0] // self.n_dp
        mine = lax.dynamic_slice_in_dim(shard, self.dp_at * rows, rows, axis=0)
        value = jnp.stack(self.round_tensor(mine), axis=0)
        return self.double(value, flip).reshape(self.n_dp, self.n_tensor, rows, shard.shape[1])

    def reduce_grad(self, grad, flip):
        _, slots, rows, cols = grad.shape
        value = grad.reshape((2,) * self.n_bits + (slots, rows, cols))
        left = list(range(self.n_bits))[::-1]
        for bit in self.orders(flip)[::-1]:
            axis = left.index(bit)
            mine = self.bit_of(bit)
            keep = lax.dynamic_index_in_dim(value, mine, axis, keepdims=False)
            send = lax.dynamic_index_in_dim(value, 1 - mine, axis, keepdims=False)
            value = (keep.astype(F32) + self.partner(send, bit).astype(F32)).astype(BF16)
            left.remove(bit)
        total = value[slots - 1]
        for slot in range(slots - 2, -1, -1):
            total = (self.turn(total, -1).astype(F32) + value[slot].astype(F32)).astype(BF16)
        return self.double(total, flip).reshape(self.n_dp * rows, cols)

    def slots(self, canonical):
        at = (self.tensor_at - jnp.arange(self.n_tensor)) % self.n_tensor
        return jnp.take(canonical, at, axis=0)


def body(
    tokens_in, norm1_gain, norm1_bias, w_qkv, bias_qv, w_out, bias_out, norm2_gain, norm2_bias,
    w_up, bias_up, w_down, bias_down, cotangent, *, n_dp, n_tensor,
):
    images, seq_len, width = tokens_in.shape
    _, _, heads, head_size = w_qkv.shape
    inner = heads * head_size
    hidden = w_up.shape[1]
    own = images // n_tensor
    assert own == 1
    rows = -(-seq_len // 128) * 128
    ring = Ring(n_dp, n_tensor)

    def own_rows(stack):
        image = lax.dynamic_index_in_dim(stack, ring.tensor_at, 0, keepdims=False)
        return jnp.pad(image, ((0, rows - seq_len), (0, 0)))

    x = own_rows(tokens_in)
    c = own_rows(cotangent)
    w_qkv_t = jnp.transpose(w_qkv, (1, 2, 3, 0)).reshape(3 * inner, width)
    wqkv = ring.gather_weight(w_qkv_t, False)
    wout = ring.gather_weight(w_out.reshape(inner, width), True)
    wup = ring.gather_weight(w_up, True)
    wdn = ring.gather_weight(w_down, False)
    biases = lax.all_gather(
        jnp.concatenate([bias_qv.reshape(2 * inner), bias_up]), "tensor", axis=0
    )
    biases = ring.slots(biases)
    bqkv = jnp.concatenate(
        [biases[:, :inner], jnp.zeros((n_tensor, inner), F32), biases[:, inner : 2 * inner]], axis=1
    )[:, None]
    bup = biases[:, None, 2 * inner :]
    vec = lambda v: v.reshape(1, width)

    row_block = whole((rows, width))
    vec_block = whole((1, width))
    act = lambda dt: jax.ShapeDtypeStruct((rows, width), dt)
    col_block = lambda n: pl.BlockSpec((rows, n), lambda g: (0, g))
    u1, qkv, o, hidden1, u2 = call(
        functools.partial(fwd_kernel, heads, head_size, seq_len),
        (n_tensor,),
        [
            row_block, vec_block, vec_block, slot_block(wqkv.shape),
            pl.BlockSpec((1, 1, 3 * inner), lambda g: (g, 0, 0)), slot_block(wout.shape),
            vec_block, vec_block, vec_block,
        ],
        [row_block, col_block(3 * inner), col_block(inner), row_block, row_block],
        [
            act(BF16), jax.ShapeDtypeStruct((rows, n_tensor * 3 * inner), BF16),
            jax.ShapeDtypeStruct((rows, n_tensor * inner), BF16), act(F32), act(BF16),
        ],
        [pltpu.VMEM((rows, width), F32)],
        "attention_forward",
    )(
        x, vec(norm1_gain), vec(norm1_bias), wqkv, bqkv, wout, vec(bias_out), vec(norm2_gain),
        vec(norm2_bias),
    )

    parts = 2
    up_block = pl.BlockSpec(
        (n_dp, 1, width // n_dp, hidden // parts), lambda g, p: (0, g, 0, p)
    )
    dn_block = pl.BlockSpec(
        (n_dp // parts, 1, hidden // n_dp, width), lambda g, p: (p, g, 0, 0)
    )
    bup_block = pl.BlockSpec((1, 1, hidden // parts), lambda g, p: (g, 0, p))
    block_own, dh1, g_up, g_dn, g_bup, small2 = call(
        mlp_kernel,
        (n_tensor, parts),
        [row_block, row_block, row_block, up_block, bup_block, dn_block, vec_block, vec_block],
        [row_block, row_block, up_block, dn_block, bup_block, whole((4, width))],
        [
            act(BF16), act(F32), jax.ShapeDtypeStruct(wup.shape, BF16),
            jax.ShapeDtypeStruct(wdn.shape, BF16), jax.ShapeDtypeStruct(bup.shape, F32),
            jax.ShapeDtypeStruct((4, width), F32),
        ],
        [pltpu.VMEM((rows, width), F32), pltpu.VMEM((rows, width), F32)],
        "mlp_both_ways",
    )(u2, hidden1, c, wup, bup, wdn, vec(bias_down), vec(norm2_gain))

    grad_own, g_qkv, g_out, g_bqkv, small1 = call(
        functools.partial(bwd_kernel, heads, head_size, seq_len),
        (n_tensor,),
        [
            row_block, vec_block, row_block, col_block(3 * inner), col_block(inner), row_block,
            slot_block(wqkv.shape), slot_block(wout.shape),
        ],
        [
            row_block, slot_block(wqkv.shape), slot_block(wout.shape),
            pl.BlockSpec((1, 1, 3 * inner), lambda g: (g, 0, 0)), whole((2, width)),
        ],
        [
            act(BF16), jax.ShapeDtypeStruct(wqkv.shape, BF16),
            jax.ShapeDtypeStruct(wout.shape, BF16), jax.ShapeDtypeStruct(bqkv.shape, F32),
            jax.ShapeDtypeStruct((2, width), F32),
        ],
        [
            pltpu.VMEM((rows, width), BF16), pltpu.VMEM((rows, width), F32),
            pltpu.VMEM((rows, 3 * inner), F32),
        ],
        "attention_backward",
    )(x, vec(norm1_gain), u1, qkv, o, dh1, wqkv, wout)

    def all_images(value):
        held = jnp.stack(ring.round_tensor(value[:seq_len]), axis=1)
        at = (ring.tensor_at - jnp.arange(n_tensor)) % n_tensor
        return jnp.transpose(jnp.take(held, at, axis=1), (1, 0, 2))

    block_out = all_images(block_own)
    grad_w_up = ring.reduce_grad(g_up, True).astype(F32)
    grad_w_down = ring.reduce_grad(g_dn, False).astype(F32)
    grad_input = all_images(grad_own).astype(F32)
    grad_w_qkv = ring.reduce_grad(g_qkv, False).astype(F32).reshape(3, heads, head_size, width)
    grad_w_qkv = jnp.transpose(grad_w_qkv, (3, 0, 1, 2))
    grad_w_out = ring.reduce_grad(g_out, True).astype(F32).reshape(heads, head_size, width)

    slot_part = jnp.concatenate(
        [g_bup[:, 0], g_bqkv[:, 0, :inner], g_bqkv[:, 0, 2 * inner :]], axis=1
    )
    packed = jnp.concatenate([small1, small2], axis=0)
    packed = lax.psum(
        jnp.concatenate([packed.reshape(-1), ring.slots(slot_part).reshape(-1)]),
        ("dp", "tensor"),
    )
    vectors = packed[: 6 * width].reshape(6, width)
    mine = lax.dynamic_index_in_dim(
        packed[6 * width :].reshape(n_tensor, -1), ring.tensor_at, 0, keepdims=False
    )
    return (
        block_out,
        grad_input,
        vectors[0],
        vectors[1],
        grad_w_qkv,
        mine[hidden:].reshape(2, heads, head_size),
        grad_w_out,
        vectors[5],
        vectors[3],
        vectors[4],
        grad_w_up,
        mine[:hidden],
        grad_w_down,
        vectors[2],
    )


def solution(mesh):
    placed = (
        P("dp", None, None),
        P(),
        P(),
        P(None, None, "tensor", None),
        P(None, "tensor", None),
        P("tensor", None, None),
        P(),
        P(),
        P(),
        P(None, "tensor"),
        P("tensor"),
        P("tensor", None),
        P(),
        P("dp", None, None),
    )
    return jax.shard_map(
        functools.partial(body, n_dp=mesh.shape["dp"], n_tensor=mesh.shape["tensor"]),
        mesh=mesh,
        in_specs=placed,
        out_specs=(
            P("dp", None, None),
            P("dp", None, None),
            P(),
            P(),
            P(None, None, "tensor", None),
            P(None, "tensor", None),
            P("tensor", None, None),
            P(),
            P(),
            P(),
            P(None, "tensor"),
            P("tensor"),
            P("tensor", None),
            P(),
        ),
        check_vma=False,
    )
```

```python
import functools

import jax
import jax.numpy as jnp
from jax import lax
from jax.experimental import pallas as pl
from jax.experimental.pallas import tpu as pltpu
from jax.sharding import PartitionSpec as P

F32 = jnp.float32
BF16 = jnp.bfloat16
EPS = 1e-06
INV_ROOT2 = 0.7071067811865476
INV_ROOT_2PI = 0.3989422804014327
LOG2E = 1.4426950408889634
VMEM_BYTES = 60 * 1024 * 1024


def mm(a, b):
    return lax.dot_general(a, b, (((1,), (0,)), ((), ())), preferred_element_type=F32)


def mm_nt(a, b):
    return lax.dot_general(a, b, (((1,), (1,)), ((), ())), preferred_element_type=F32)


def mm_tn(a, b):
    return lax.dot_general(a, b, (((0,), (0,)), ((), ())), preferred_element_type=F32)


def whiten(values):
    centred = values - jnp.mean(values, axis=-1, keepdims=True)
    inv_std = lax.rsqrt(jnp.mean(centred * centred, axis=-1, keepdims=True) + EPS)
    return centred * inv_std, inv_std


def norm_back(grad_out, white, inv_std, gain):
    grad_white = grad_out * gain
    inner = (
        grad_white
        - jnp.mean(grad_white, axis=-1, keepdims=True)
        - white * jnp.mean(grad_white * white, axis=-1, keepdims=True)
    )
    return inv_std * inner


def row_sum(values):
    return jnp.sum(values, axis=0, keepdims=True)


def joined(ref):
    block = ref[...]
    return block.reshape(block.shape[0] * block.shape[2], block.shape[3])


def weights_of_slot(at_ref, near, far, split, qkv_ref, out_ref):
    cut = qkv_ref.shape[1]
    for refs, wanted in ((near, pl.program_id(0) < split), (far, pl.program_id(0) >= split)):

        @pl.when(wanted)
        def _(refs=refs):
            for distance, ref in enumerate(refs):
                place = at_ref[0] ^ distance
                qkv_ref[place] = ref[0, :cut]
                out_ref[place] = ref[0, cut:]


def merged(ref):
    block = ref[...]
    return block.reshape(block.shape[0] * block.shape[1], block.shape[2])


def fwd_kernel(n_dp, split, heads, head_size, tokens, at_ref, *refs):
    near, far = refs[:n_dp], refs[n_dp : 2 * n_dp]
    (
        x_ref, g1_ref, b1_ref, bqkv_ref, bout_ref, g2_ref, b2_ref,
        u1_ref, qkv_ref, o_ref, h1_ref, u2_ref, acc_ref, wqkv_ref, wout_ref,
    ) = refs[2 * n_dp :]
    step = pl.program_id(0)
    weights_of_slot(at_ref, near, far, split, wqkv_ref, wout_ref)

    @pl.when(step == 0)
    def _():
        white, _ = whiten(x_ref[...].astype(F32))
        u1_ref[...] = (white * g1_ref[...] + b1_ref[...]).astype(BF16)
        acc_ref[...] = jnp.zeros_like(acc_ref)

    qkv = (mm_nt(u1_ref[...], merged(wqkv_ref)) + bqkv_ref[0]).astype(BF16)
    qkv_ref[...] = qkv
    inner = heads * head_size
    rows = qkv.shape[0]
    factor = LOG2E * head_size ** (-0.5)
    real = lax.broadcasted_iota(jnp.int32, (1, rows), 1) < tokens
    outs = []
    for head in range(heads):
        q = qkv[:, head * head_size : (head + 1) * head_size]
        k = qkv[:, inner + head * head_size : inner + (head + 1) * head_size]
        v = qkv[:, 2 * inner + head * head_size : 2 * inner + (head + 1) * head_size]
        scores = jnp.where(real, mm_nt(q, k) * factor, -1e30)
        expos = jnp.exp2(scores - jnp.max(scores, axis=-1, keepdims=True))
        total = jnp.sum(expos, axis=-1, keepdims=True)
        outs.append((mm(expos.astype(BF16), v) / total).astype(BF16))
    o = jnp.concatenate(outs, axis=1)
    o_ref[...] = o
    acc_ref[...] += mm(o, merged(wout_ref))

    @pl.when(step == pl.num_programs(0) - 1)
    def _():
        hidden1 = x_ref[...].astype(F32) + acc_ref[...] + bout_ref[...]
        h1_ref[...] = hidden1
        white, _ = whiten(hidden1)
        u2_ref[...] = (white * g2_ref[...] + b2_ref[...]).astype(BF16)


def mlp_kernel(
    parts, u2_ref, h1_ref, c_ref, wup_ref, bup_ref, wdn_ref, bdn_ref, g2_ref,
    out_ref, dh1_ref, gw_ref, gbup_ref, small_ref, acc_ref, dacc_ref,
):
    part = pl.program_id(1)
    step = pl.program_id(0) * parts + part

    @pl.when(step == 0)
    def _():
        acc_ref[...] = jnp.zeros_like(acc_ref)
        dacc_ref[...] = jnp.zeros_like(dacc_ref)

    u2 = u2_ref[...]
    c = c_ref[...]
    wup = joined(wup_ref)
    wdn = joined(wdn_ref)
    pre = mm(u2, wup) + bup_ref[0]
    half = 0.5 * (1.0 + lax.erf(pre * INV_ROOT2))
    hid = (pre * half).astype(BF16)
    slope = half + pre * INV_ROOT_2PI * jnp.exp(-0.5 * pre * pre)
    acc_ref[...] += mm(hid, wdn)
    up_rows, dn_rows = wup_ref.shape[2], wdn_ref.shape[2]
    gdn = mm_tn(hid, c).astype(BF16).reshape(wdn_ref.shape[0], dn_rows, c.shape[1])
    dpre = mm_nt(c, wdn) * slope
    gbup_ref[0] = row_sum(dpre)
    dpre_bf = dpre.astype(BF16)
    gup = mm_tn(u2, dpre_bf).astype(BF16).reshape(wup_ref.shape[0], up_rows, hid.shape[1])
    for at in range(parts):

        @pl.when(part == at)
        def _(at=at):
            span, cols = wdn_ref.shape[0], hid.shape[1]
            gw_ref[at * span : (at + 1) * span, 0, up_rows:, :] = gdn
            gw_ref[:, 0, :up_rows, at * cols : (at + 1) * cols] = gup

    dacc_ref[...] += mm_nt(dpre_bf, wup)

    @pl.when(step == pl.num_programs(0) * parts - 1)
    def _():
        hidden1 = h1_ref[...]
        out = (hidden1 + acc_ref[...] + bdn_ref[...]).astype(BF16)
        out_ref[...] = out[: out_ref.shape[0]]
        white, inv_std = whiten(hidden1)
        du2 = dacc_ref[...]
        cf = c.astype(F32)
        dh1 = cf + norm_back(du2, white, inv_std, g2_ref[...])
        dh1_ref[...] = dh1
        small_ref[...] = jnp.concatenate(
            [row_sum(cf), row_sum(du2 * white), row_sum(du2), row_sum(dh1)], axis=0
        )


def bwd_kernel(n_dp, split, heads, head_size, tokens, at_ref, *refs):
    near, far = refs[:n_dp], refs[n_dp : 2 * n_dp]
    (
        x_ref, g1_ref, u1_ref, qkv_ref, o_ref, dh1_ref,
        gin_ref, keep_ref, send_ref, gbias_ref, small_ref,
        dhb_ref, acc_ref, dqkv_ref, wqkv_ref, wout_ref,
    ) = refs[2 * n_dp :]
    step = pl.program_id(0)
    weights_of_slot(at_ref, near, far, split, wqkv_ref, wout_ref)

    @pl.when(step == 0)
    def _():
        dhb_ref[...] = dh1_ref[...].astype(BF16)
        acc_ref[...] = jnp.zeros_like(acc_ref)

    dhb = dhb_ref[...]
    qkv = qkv_ref[...]
    up = mm_nt(dhb, merged(wout_ref)).astype(BF16)
    inner = heads * head_size
    rows = qkv.shape[0]
    scale = head_size ** (-0.5)
    real = lax.broadcasted_iota(jnp.int32, (rows, 1), 0) < tokens
    for head in range(heads):
        q = qkv[:, head * head_size : (head + 1) * head_size]
        k = qkv[:, inner + head * head_size : inner + (head + 1) * head_size]
        v = qkv[:, 2 * inner + head * head_size : 2 * inner + (head + 1) * head_size]
        do = up[:, head * head_size : (head + 1) * head_size]
        scores = jnp.where(real, mm_nt(k, q) * (LOG2E * scale), -1e30)
        expos = jnp.exp2(scores - jnp.max(scores, axis=0, keepdims=True))
        probs = expos * (1.0 / jnp.sum(expos, axis=0, keepdims=True))
        dv = mm(probs.astype(BF16), do)
        dprob = mm_nt(v, do)
        delta = jnp.sum(probs * dprob, axis=0, keepdims=True)
        dscore = (probs * (dprob - delta) * scale).astype(BF16)
        dk = mm(dscore, q)
        dq = mm_tn(dscore, k)
        dqkv_ref[:, head * head_size : (head + 1) * head_size] = dq
        dqkv_ref[:, inner + head * head_size : inner + (head + 1) * head_size] = dk
        dqkv_ref[:, 2 * inner + head * head_size : 2 * inner + (head + 1) * head_size] = dv
    dqkv = dqkv_ref[...]
    gbias_ref[0] = row_sum(dqkv)
    dqkv_bf = dqkv.astype(BF16)
    acc_ref[...] += mm(dqkv_bf, merged(wqkv_ref))
    wqkv_ref[...] = mm_tn(dqkv_bf, u1_ref[...]).astype(BF16).reshape(wqkv_ref.shape)
    wout_ref[...] = mm_tn(o_ref[...], dhb).astype(BF16).reshape(wout_ref.shape)
    cut = wqkv_ref.shape[1]
    for distance in range(n_dp):
        place = at_ref[0] ^ distance
        ref = send_ref if distance & 1 else keep_ref
        ref[distance >> 1, 0, :cut] = wqkv_ref[place]
        ref[distance >> 1, 0, cut:] = wout_ref[place]

    @pl.when(step == pl.num_programs(0) - 1)
    def _():
        white, inv_std = whiten(x_ref[...].astype(F32))
        du1 = acc_ref[...]
        gin = (dh1_ref[...] + norm_back(du1, white, inv_std, g1_ref[...])).astype(BF16)
        gin_ref[...] = gin[: gin_ref.shape[0]]
        small_ref[...] = jnp.concatenate([row_sum(du1 * white), row_sum(du1)], axis=0)


def order_kernel(n_dp, at_ref, *refs):
    first_ref, second_ref = refs[n_dp:]
    cut = first_ref.shape[1]
    for distance in range(n_dp):
        place = at_ref[0] ^ distance
        first_ref[place] = refs[distance][:cut].astype(F32)
        second_ref[place] = refs[distance][cut:].astype(F32)


def whole(shape):
    return pl.BlockSpec(shape, lambda *_: (0,) * len(shape))


def call(kernel, grid, in_specs, out_specs, out_shape, scratch, name, scalars=0):
    return pl.pallas_call(
        kernel,
        grid_spec=pltpu.PrefetchScalarGridSpec(
            num_scalar_prefetch=scalars,
            grid=grid,
            in_specs=in_specs,
            out_specs=out_specs,
            scratch_shapes=scratch,
        ),
        out_shape=out_shape,
        compiler_params=pltpu.CompilerParams(
            dimension_semantics=("arbitrary",) * len(grid), vmem_limit_bytes=VMEM_BYTES
        ),
        name=name,
    )


def add(left, right):
    return (left.astype(F32) + right.astype(F32)).astype(BF16)


class Ring:
    def __init__(self, n_dp, n_tensor):
        self.n_dp = n_dp
        self.n_tensor = n_tensor
        self.n_bits = n_dp.bit_length() - 1
        assert 1 << self.n_bits == n_dp
        self.dp_at = lax.axis_index("dp")
        self.tensor_at = lax.axis_index("tensor")

    def turn(self, value, by):
        pairs = [(i, (i + by) % self.n_tensor) for i in range(self.n_tensor)]
        return lax.ppermute(value, "tensor", pairs)

    def partner(self, value, bit):
        return lax.ppermute(value, "dp", [(i, i ^ (1 << bit)) for i in range(self.n_dp)])

    def outer_bits(self, flip):
        bits = list(range(1, self.n_bits))
        return bits[::-1] if flip else bits

    def round_tensor(self, value):
        held = [value]
        for _ in range(self.n_tensor - 1):
            held.append(self.turn(held[-1], 1))
        return held

    def spread(self, value, flip):
        pieces = {0: value}
        for bit in self.outer_bits(flip) + [0]:
            for distance in list(pieces):
                pieces[distance | 1 << bit] = self.partner(pieces[distance], bit)
        return [pieces[distance] for distance in range(self.n_dp)]

    def part_of(self, shard):
        rows = shard.shape[0] // self.n_dp
        return lax.dynamic_slice_in_dim(shard, self.dp_at * rows, rows, axis=0)

    def gather_slots(self, mine):
        held = self.round_tensor(mine)
        split = self.n_tensor // 2
        near = self.spread(jnp.stack(held[:split]), False)
        far = self.spread(jnp.stack(held[split:]), True)
        return near, far

    def reduce_slots(self, keep, send):
        other = self.partner(send, 0)
        split = self.n_tensor // 2
        halves = []
        for flip, low, high in ((False, 0, split), (True, split, self.n_tensor)):
            held = {q: add(keep[q, low:high], other[q, low:high]) for q in range(self.n_dp // 2)}
            for bit in self.outer_bits(flip):
                mask = 1 << (bit - 1)
                held = {
                    q: add(held[q], self.partner(held[q | mask], bit))
                    for q in held
                    if not q & mask
                }
            halves.append(held[0])
        slot = lambda j: halves[0][j] if j < split else halves[1][j - split]
        total = slot(self.n_tensor - 1)
        for j in range(self.n_tensor - 2, -1, -1):
            total = add(self.turn(total, -1), slot(j))
        return total

    def slots(self, canonical):
        at = (self.tensor_at - jnp.arange(self.n_tensor)) % self.n_tensor
        return jnp.take(canonical, at, axis=0)

    def sum_all(self, value):
        for bit in range(self.n_bits):
            value = value + self.partner(value, bit)
        held = self.slots(jnp.stack(self.round_tensor(value)))
        total = held[0]
        for j in range(1, self.n_tensor):
            total = total + held[j]
        return total

    def all_images(self, value, dtype):
        held = self.round_tensor(value)
        images = []
        for image in range(self.n_tensor):
            back = (self.tensor_at - image) % self.n_tensor
            chosen = held[0]
            for j in range(1, self.n_tensor):
                chosen = jnp.where(back == j, held[j], chosen)
            images.append(chosen.astype(dtype))
        return jnp.transpose(jnp.stack(images, axis=1), (1, 0, 2))


def body(
    tokens_in, norm1_gain, norm1_bias, w_qkv, bias_qv, w_out, bias_out, norm2_gain, norm2_bias,
    w_up, bias_up, w_down, bias_down, cotangent, *, n_dp, n_tensor,
):
    images, seq_len, width = tokens_in.shape
    _, _, heads, head_size = w_qkv.shape
    inner = heads * head_size
    hidden = w_up.shape[1]
    assert images == n_tensor
    rows = -(-seq_len // 128) * 128
    ring = Ring(n_dp, n_tensor)
    at = jnp.stack([ring.dp_at, ring.tensor_at]).astype(jnp.int32)

    w_qkv_t = jnp.transpose(w_qkv, (1, 2, 3, 0)).reshape(3 * inner, width)
    cut = 3 * inner // n_dp
    attn_part = jnp.concatenate(
        [ring.part_of(w_qkv_t), ring.part_of(w_out.reshape(inner, width))], axis=0
    )
    attn_rows = attn_part.shape[0]
    near, far = ring.gather_slots(attn_part)
    mlp_part = jnp.concatenate([ring.part_of(w_up), ring.part_of(w_down)], axis=0)
    mlp_rows = mlp_part.shape[0]
    wmlp = lax.all_gather(mlp_part, ("dp", "tensor"), axis=0)
    wmlp = wmlp.reshape(n_dp, n_tensor, mlp_rows, width)

    def own_rows(stack):
        image = lax.dynamic_index_in_dim(stack, ring.tensor_at, 0, keepdims=False)
        return jnp.pad(image, ((0, rows - seq_len), (0, 0)))

    x = own_rows(tokens_in)
    c = own_rows(cotangent)
    biases = jnp.concatenate([bias_qv.reshape(2 * inner), bias_up])
    biases = jnp.stack(ring.round_tensor(biases.reshape(-1, 128))).reshape(n_tensor, -1)
    bqkv = jnp.concatenate(
        [biases[:, :inner], jnp.zeros((n_tensor, inner), F32), biases[:, inner : 2 * inner]], axis=1
    )[:, None]
    bup = ring.slots(biases[:, 2 * inner :])[:, None]
    vec = lambda v: v.reshape(1, width)

    row_block = whole((rows, width))
    vec_block = whole((1, width))
    act = lambda dt: jax.ShapeDtypeStruct((rows, width), dt)
    col_block = lambda n: pl.BlockSpec((rows, n), lambda g, *_: (0, g))
    slot_row = pl.BlockSpec((1, 1, 3 * inner), lambda g, *_: (g, 0, 0))
    split = n_tensor // 2
    near_block = pl.BlockSpec(
        (1, attn_rows, width), lambda g, *_: (jnp.minimum(g, split - 1), 0, 0)
    )
    far_block = pl.BlockSpec(
        (1, attn_rows, width), lambda g, *_: (jnp.maximum(g - split, 0), 0, 0)
    )
    piece_blocks = [near_block] * n_dp + [far_block] * n_dp
    weight_scratch = [
        pltpu.VMEM((n_dp, cut, width), BF16),
        pltpu.VMEM((n_dp, attn_rows - cut, width), BF16),
    ]
    u1, qkv, o, hidden1, u2 = call(
        functools.partial(fwd_kernel, n_dp, split, heads, head_size, seq_len),
        (n_tensor,),
        piece_blocks
        + [row_block, vec_block, vec_block, slot_row, vec_block, vec_block, vec_block],
        [row_block, col_block(3 * inner), col_block(inner), row_block, row_block],
        [
            act(BF16), jax.ShapeDtypeStruct((rows, n_tensor * 3 * inner), BF16),
            jax.ShapeDtypeStruct((rows, n_tensor * inner), BF16), act(F32), act(BF16),
        ],
        [pltpu.VMEM((rows, width), F32)] + weight_scratch,
        "attention_forward",
        1,
    )(
        at, *near, *far, x, vec(norm1_gain), vec(norm1_bias), bqkv, vec(bias_out),
        vec(norm2_gain), vec(norm2_bias),
    )

    parts = 2
    up_block = pl.BlockSpec((n_dp, 1, width // n_dp, hidden // parts), lambda g, p: (0, g, 0, p))
    dn_block = pl.BlockSpec((n_dp // parts, 1, hidden // n_dp, width), lambda g, p: (p, g, 1, 0))
    bup_block = pl.BlockSpec((1, 1, hidden // parts), lambda g, p: (g, 0, p))
    image_block = whole((seq_len, width))
    image = jax.ShapeDtypeStruct((seq_len, width), BF16)
    block_own, dh1, g_mlp, g_bup, small2 = call(
        functools.partial(mlp_kernel, parts),
        (n_tensor, parts),
        [row_block, row_block, row_block, up_block, bup_block, dn_block, vec_block, vec_block],
        [
            image_block, row_block,
            pl.BlockSpec((n_dp, 1, mlp_rows, width), lambda g, p: (0, g, 0, 0)),
            bup_block, whole((4, width)),
        ],
        [
            image, act(F32), jax.ShapeDtypeStruct(wmlp.shape, BF16),
            jax.ShapeDtypeStruct(bup.shape, F32), jax.ShapeDtypeStruct((4, width), F32),
        ],
        [pltpu.VMEM((rows, width), F32), pltpu.VMEM((rows, width), F32)],
        "mlp_both_ways",
    )(u2, hidden1, c, wmlp, bup, wmlp, vec(bias_down), vec(norm2_gain))

    mlp_total = lax.psum_scatter(
        g_mlp.reshape(n_dp * n_tensor, mlp_rows, width), ("dp", "tensor"), scatter_dimension=0
    )

    grad_block = pl.BlockSpec((n_dp // 2, 1, attn_rows, width), lambda g, *_: (0, g, 0, 0))
    grad_shape = jax.ShapeDtypeStruct((n_dp // 2, n_tensor, attn_rows, width), BF16)
    grad_own, keep, send, g_bqkv, small1 = call(
        functools.partial(bwd_kernel, n_dp, split, heads, head_size, seq_len),
        (n_tensor,),
        piece_blocks
        + [row_block, vec_block, row_block, col_block(3 * inner), col_block(inner), row_block],
        [image_block, grad_block, grad_block, slot_row, whole((2, width))],
        [
            image, grad_shape, grad_shape, jax.ShapeDtypeStruct(bqkv.shape, F32),
            jax.ShapeDtypeStruct((2, width), F32),
        ],
        [
            pltpu.VMEM((rows, width), BF16), pltpu.VMEM((rows, width), F32),
            pltpu.VMEM((rows, 3 * inner), F32),
        ]
        + weight_scratch,
        "attention_backward",
        1,
    )(at, *near, *far, x, vec(norm1_gain), u1, qkv, o, dh1)

    def ordered(piece, first_rows, flip, name):
        n_rows = piece.shape[0]
        shapes = [(n_dp, first_rows, width), (n_dp, n_rows - first_rows, width)]
        first, second = call(
            functools.partial(order_kernel, n_dp),
            (1,),
            [whole((n_rows, width))] * n_dp,
            [whole(shape) for shape in shapes],
            [jax.ShapeDtypeStruct(shape, F32) for shape in shapes],
            [],
            name,
            1,
        )(at, *ring.spread(piece, flip))
        return first.reshape(-1, width), second.reshape(-1, width)

    block_out = ring.all_images(block_own, BF16)
    grad_input = ring.all_images(grad_own, F32)
    attn_total = ring.reduce_slots(keep, send)
    grad_w_qkv, grad_w_out = ordered(attn_total, cut, True, "order_attention")
    grad_w_up, grad_w_down = ordered(mlp_total, width // n_dp, False, "order_mlp")
    grad_w_qkv = jnp.transpose(grad_w_qkv.reshape(3, heads, head_size, width), (3, 0, 1, 2))
    grad_w_out = grad_w_out.reshape(heads, head_size, width)

    g_bqkv = ring.slots(g_bqkv[:, 0])
    slot_part = jnp.concatenate(
        [g_bup[:, 0], g_bqkv[:, :inner], g_bqkv[:, 2 * inner :]], axis=1
    )
    packed = jnp.concatenate([small1.reshape(-1), small2.reshape(-1), slot_part.reshape(-1)])
    packed = ring.sum_all(packed.reshape(-1, 128)).reshape(-1)
    vectors = packed[: 6 * width].reshape(6, width)
    mine = lax.dynamic_index_in_dim(
        packed[6 * width :].reshape(n_tensor, -1), ring.tensor_at, 0, keepdims=False
    )
    return (
        block_out,
        grad_input,
        vectors[0],
        vectors[1],
        grad_w_qkv,
        mine[hidden:].reshape(2, heads, head_size),
        grad_w_out,
        vectors[5],
        vectors[3],
        vectors[4],
        grad_w_up,
        mine[:hidden],
        grad_w_down,
        vectors[2],
    )


def solution(mesh):
    placed = (
        P("dp", None, None),
        P(),
        P(),
        P(None, None, "tensor", None),
        P(None, "tensor", None),
        P("tensor", None, None),
        P(),
        P(),
        P(),
        P(None, "tensor"),
        P("tensor"),
        P("tensor", None),
        P(),
        P("dp", None, None),
    )
    return jax.shard_map(
        functools.partial(body, n_dp=mesh.shape["dp"], n_tensor=mesh.shape["tensor"]),
        mesh=mesh,
        in_specs=placed,
        out_specs=(
            P("dp", None, None),
            P("dp", None, None),
            P(),
            P(),
            P(None, None, "tensor", None),
            P(None, "tensor", None),
            P("tensor", None, None),
            P(),
            P(),
            P(),
            P(None, "tensor"),
            P("tensor"),
            P("tensor", None),
            P(),
        ),
        check_vma=False,
    )
```

```python
import functools

import jax
import jax.numpy as jnp
from jax import lax
from jax.experimental import pallas as pl
from jax.experimental.pallas import tpu as pltpu
from jax.sharding import PartitionSpec as P

F32 = jnp.float32
BF16 = jnp.bfloat16
EPS = 1e-06
INV_ROOT2 = 0.7071067811865476
INV_ROOT_2PI = 0.3989422804014327
LOG2E = 1.4426950408889634
VMEM_BYTES = 60 * 1024 * 1024


def mm(a, b):
    return lax.dot_general(a, b, (((1,), (0,)), ((), ())), preferred_element_type=F32)


def mm_nt(a, b):
    return lax.dot_general(a, b, (((1,), (1,)), ((), ())), preferred_element_type=F32)


def mm_tn(a, b):
    return lax.dot_general(a, b, (((0,), (0,)), ((), ())), preferred_element_type=F32)


def whiten(values):
    centred = values - jnp.mean(values, axis=-1, keepdims=True)
    inv_std = lax.rsqrt(jnp.mean(centred * centred, axis=-1, keepdims=True) + EPS)
    return centred * inv_std, inv_std


def norm_back(grad_out, white, inv_std, gain):
    grad_white = grad_out * gain
    inner = (
        grad_white
        - jnp.mean(grad_white, axis=-1, keepdims=True)
        - white * jnp.mean(grad_white * white, axis=-1, keepdims=True)
    )
    return inv_std * inner


def row_sum(values):
    return jnp.sum(values, axis=0, keepdims=True)


def joined(ref):
    block = ref[...]
    return block.reshape(block.shape[0] * block.shape[2], block.shape[3])


def weights_of_slot(at_ref, refs, qkv_ref, out_ref):
    cut = qkv_ref.shape[1]
    for distance, ref in enumerate(refs):
        place = at_ref[0] ^ distance
        qkv_ref[place] = ref[0, :cut]
        out_ref[place] = ref[0, cut:]


def merged(ref):
    block = ref[...]
    return block.reshape(block.shape[0] * block.shape[1], block.shape[2])


def fwd_kernel(n_dp, split, heads, head_size, tokens, at_ref, *refs):
    near, far = refs[:n_dp], refs[n_dp : 2 * n_dp]
    (
        x_ref, g1_ref, b1_ref, bqkv_ref, bout_ref, g2_ref, b2_ref,
        u1_ref, qkv_ref, o_ref, h1_ref, u2_ref, acc_ref, wqkv_ref, wout_ref,
    ) = refs[2 * n_dp :]
    step = pl.program_id(0)

    @pl.when(step < split)
    def _():
        weights_of_slot(at_ref, near, wqkv_ref, wout_ref)

    @pl.when(step >= split)
    def _():
        weights_of_slot(at_ref, far, wqkv_ref, wout_ref)

    @pl.when(step == 0)
    def _():
        white, _ = whiten(x_ref[...].astype(F32))
        u1_ref[...] = (white * g1_ref[...] + b1_ref[...]).astype(BF16)
        acc_ref[...] = jnp.zeros_like(acc_ref)

    qkv = (mm_nt(u1_ref[...], merged(wqkv_ref)) + bqkv_ref[0]).astype(BF16)
    qkv_ref[...] = qkv
    inner = heads * head_size
    rows = qkv.shape[0]
    factor = LOG2E * head_size ** (-0.5)
    real = lax.broadcasted_iota(jnp.int32, (1, rows), 1) < tokens
    outs = []
    for head in range(heads):
        q = qkv[:, head * head_size : (head + 1) * head_size]
        k = qkv[:, inner + head * head_size : inner + (head + 1) * head_size]
        v = qkv[:, 2 * inner + head * head_size : 2 * inner + (head + 1) * head_size]
        scores = jnp.where(real, mm_nt(q, k) * factor, -1e30)
        expos = jnp.exp2(scores - jnp.max(scores, axis=-1, keepdims=True))
        total = jnp.sum(expos, axis=-1, keepdims=True)
        outs.append((mm(expos.astype(BF16), v) / total).astype(BF16))
    o = jnp.concatenate(outs, axis=1)
    o_ref[...] = o
    acc_ref[...] += mm(o, merged(wout_ref))

    @pl.when(step == pl.num_programs(0) - 1)
    def _():
        hidden1 = x_ref[...].astype(F32) + acc_ref[...] + bout_ref[...]
        h1_ref[...] = hidden1
        white, _ = whiten(hidden1)
        u2_ref[...] = (white * g2_ref[...] + b2_ref[...]).astype(BF16)


def mlp_fwd_kernel(
    parts, at_ref, u2_ref, wup_ref, bup_ref, wdn_ref, h1_ref, bdn_ref, pre_ref, out_ref, acc_ref
):
    step = pl.program_id(0) * parts + pl.program_id(1)

    @pl.when(step == 0)
    def _():
        acc_ref[...] = jnp.zeros_like(acc_ref)

    pre = mm(u2_ref[...], joined(wup_ref)) + bup_ref[0]
    pre_ref[...] = pre
    hid = (0.5 * pre * (1.0 + lax.erf(pre * INV_ROOT2))).astype(BF16)
    acc_ref[...] += mm(hid, joined(wdn_ref))

    @pl.when(step == pl.num_programs(0) * parts - 1)
    def _():
        out = (h1_ref[...] + acc_ref[...] + bdn_ref[...]).astype(BF16)
        out_ref[...] = out[: out_ref.shape[0]]


def mlp_kernel(parts, last, at_ref, u2_ref, c_ref, wup_ref, pre_ref, wdn_ref, *refs):
    if last:
        (
            h1_ref, g2_ref, dacc_in,
            keep_ref, send_ref, gbup_ref, dh1_ref, small_ref, gw_ref, dacc_ref,
        ) = refs
    else:
        keep_ref, send_ref, gbup_ref, dacc_ref, gw_ref = refs
    part = pl.program_id(1)
    step = pl.program_id(0) * parts + part

    @pl.when(step == 0)
    def _():
        dacc_ref[...] = dacc_in[...] if last else jnp.zeros_like(dacc_ref)

    u2 = u2_ref[...]
    c = c_ref[...]
    pre = pre_ref[...]
    half = 0.5 * (1.0 + lax.erf(pre * INV_ROOT2))
    hid = (pre * half).astype(BF16)
    slope = half + pre * INV_ROOT_2PI * jnp.exp(-0.5 * pre * pre)
    up_rows, dn_rows = wup_ref.shape[2], wdn_ref.shape[2]
    gdn = mm_tn(hid, c).astype(BF16).reshape(wdn_ref.shape[0], dn_rows, c.shape[1])
    dpre = mm_nt(c, joined(wdn_ref)) * slope
    gbup_ref[0] = row_sum(dpre)
    dpre_bf = dpre.astype(BF16)
    gup = mm_tn(u2, dpre_bf).astype(BF16).reshape(wup_ref.shape[0], up_rows, hid.shape[1])
    for at in range(parts):

        @pl.when(part == at)
        def _(at=at):
            span, cols = wdn_ref.shape[0], hid.shape[1]
            gw_ref[at * span : (at + 1) * span, up_rows:, :] = gdn
            gw_ref[:, :up_rows, at * cols : (at + 1) * cols] = gup

    @pl.when(part == parts - 1)
    def _():
        for distance in range(gw_ref.shape[0]):
            ref = send_ref if distance & 1 else keep_ref
            ref[distance >> 1, 0] = gw_ref[at_ref[0] ^ distance]

    dacc_ref[...] += mm_nt(dpre_bf, joined(wup_ref))
    if not last:
        return

    @pl.when(step == pl.num_programs(0) * parts - 1)
    def _():
        white, inv_std = whiten(h1_ref[...])
        du2 = dacc_ref[...]
        cf = c.astype(F32)
        dh1 = cf + norm_back(du2, white, inv_std, g2_ref[...])
        dh1_ref[...] = dh1
        small_ref[...] = jnp.concatenate(
            [row_sum(cf), row_sum(du2 * white), row_sum(du2), row_sum(dh1)], axis=0
        )


def bwd_kernel(n_dp, last, heads, head_size, tokens, at_ref, *refs):
    pieces = refs[:n_dp]
    u1_ref, qkv_ref, o_ref, dh1_ref = refs[n_dp : n_dp + 4]
    if last:
        (
            x_ref, g1_ref, acc_in, keep_ref, send_ref, gbias_ref, gin_ref, small_ref,
            dhb_ref, dqkv_ref, wqkv_ref, wout_ref, acc_ref,
        ) = refs[n_dp + 4 :]
    else:
        (
            keep_ref, send_ref, gbias_ref, acc_ref, dhb_ref, dqkv_ref, wqkv_ref, wout_ref,
        ) = refs[n_dp + 4 :]
    step = pl.program_id(0)
    weights_of_slot(at_ref, pieces, wqkv_ref, wout_ref)

    @pl.when(step == 0)
    def _():
        dhb_ref[...] = dh1_ref[...].astype(BF16)
        acc_ref[...] = acc_in[...] if last else jnp.zeros_like(acc_ref)

    dhb = dhb_ref[...]
    qkv = qkv_ref[...]
    up = mm_nt(dhb, merged(wout_ref)).astype(BF16)
    inner = heads * head_size
    rows = qkv.shape[0]
    scale = head_size ** (-0.5)
    real = lax.broadcasted_iota(jnp.int32, (rows, 1), 0) < tokens
    for head in range(heads):
        q = qkv[:, head * head_size : (head + 1) * head_size]
        k = qkv[:, inner + head * head_size : inner + (head + 1) * head_size]
        v = qkv[:, 2 * inner + head * head_size : 2 * inner + (head + 1) * head_size]
        do = up[:, head * head_size : (head + 1) * head_size]
        scores = jnp.where(real, mm_nt(k, q) * (LOG2E * scale), -1e30)
        expos = jnp.exp2(scores - jnp.max(scores, axis=0, keepdims=True))
        probs = expos * (1.0 / jnp.sum(expos, axis=0, keepdims=True))
        dv = mm(probs.astype(BF16), do)
        dprob = mm_nt(v, do)
        delta = jnp.sum(probs * dprob, axis=0, keepdims=True)
        dscore = (probs * (dprob - delta) * scale).astype(BF16)
        dk = mm(dscore, q)
        dq = mm_tn(dscore, k)
        dqkv_ref[:, head * head_size : (head + 1) * head_size] = dq
        dqkv_ref[:, inner + head * head_size : inner + (head + 1) * head_size] = dk
        dqkv_ref[:, 2 * inner + head * head_size : 2 * inner + (head + 1) * head_size] = dv
    dqkv = dqkv_ref[...]
    gbias_ref[0] = row_sum(dqkv)
    dqkv_bf = dqkv.astype(BF16)
    acc_ref[...] += mm(dqkv_bf, merged(wqkv_ref))
    wqkv_ref[...] = mm_tn(dqkv_bf, u1_ref[...]).astype(BF16).reshape(wqkv_ref.shape)
    wout_ref[...] = mm_tn(o_ref[...], dhb).astype(BF16).reshape(wout_ref.shape)
    cut = wqkv_ref.shape[1]
    for distance in range(n_dp):
        place = at_ref[0] ^ distance
        ref = send_ref if distance & 1 else keep_ref
        ref[distance >> 1, 0, :cut] = wqkv_ref[place]
        ref[distance >> 1, 0, cut:] = wout_ref[place]
    if not last:
        return

    @pl.when(step == pl.num_programs(0) - 1)
    def _():
        white, inv_std = whiten(x_ref[...].astype(F32))
        du1 = acc_ref[...]
        gin = (dh1_ref[...] + norm_back(du1, white, inv_std, g1_ref[...])).astype(BF16)
        gin_ref[...] = gin[: gin_ref.shape[0]]
        small_ref[...] = jnp.concatenate([row_sum(du1 * white), row_sum(du1)], axis=0)


def order_kernel(places, at_ref, mine_ref, other_ref, first_ref, second_ref):
    cut = first_ref.shape[1]
    for ref, low in ((mine_ref, 0), (other_ref, 1)):
        for index, distance in enumerate(places):
            place = at_ref[0] ^ (distance | low)
            first_ref[place] = ref[index, :cut].astype(F32)
            second_ref[place] = ref[index, cut:].astype(F32)


def images_kernel(spans, at_ref, *refs):
    out_ref = refs[-1]
    count = out_ref.shape[1]
    for index, (low, high) in enumerate(spans):
        held = refs[index * count : (index + 1) * count]
        for image in range(count):
            back = lax.rem(at_ref[1] - image + count, count)
            chosen = held[0][...]
            for j in range(1, count):
                chosen = jnp.where(back == j, held[j][...], chosen)
            out_ref[:, image, low:high] = chosen.astype(out_ref.dtype)


def whole(shape):
    return pl.BlockSpec(shape, lambda *_: (0,) * len(shape))


def call(kernel, grid, in_specs, out_specs, out_shape, scratch, name, scalars=0):
    return pl.pallas_call(
        kernel,
        grid_spec=pltpu.PrefetchScalarGridSpec(
            num_scalar_prefetch=scalars,
            grid=grid,
            in_specs=in_specs,
            out_specs=out_specs,
            scratch_shapes=scratch,
        ),
        out_shape=out_shape,
        compiler_params=pltpu.CompilerParams(
            dimension_semantics=("arbitrary",) * len(grid), vmem_limit_bytes=VMEM_BYTES
        ),
        name=name,
    )


def add(left, right):
    return (left.astype(F32) + right.astype(F32)).astype(BF16)


class Ring:
    def __init__(self, n_dp, n_tensor):
        self.n_dp = n_dp
        self.n_tensor = n_tensor
        self.n_bits = n_dp.bit_length() - 1
        assert 1 << self.n_bits == n_dp
        self.dp_at = lax.axis_index("dp")
        self.tensor_at = lax.axis_index("tensor")

    def turn(self, value, by):
        pairs = [(i, (i + by) % self.n_tensor) for i in range(self.n_tensor)]
        return lax.ppermute(value, "tensor", pairs)

    def partner(self, value, bit):
        return lax.ppermute(value, "dp", [(i, i ^ (1 << bit)) for i in range(self.n_dp)])

    def outer_bits(self, flip):
        bits = list(range(1, self.n_bits))
        return bits[::-1] if flip else bits

    def round_tensor(self, value):
        held = [value]
        for _ in range(self.n_tensor - 1):
            held.append(self.turn(held[-1], 1))
        return held

    def spread(self, value, flip):
        pieces = {0: value}
        for bit in self.outer_bits(flip) + [0]:
            for distance in list(pieces):
                pieces[distance | 1 << bit] = self.partner(pieces[distance], bit)
        return [pieces[distance] for distance in range(self.n_dp)]

    def part_of(self, shard):
        rows = shard.shape[0] // self.n_dp
        return lax.dynamic_slice_in_dim(shard, self.dp_at * rows, rows, axis=0)

    def gather_slots(self, mine):
        held = self.round_tensor(mine)
        split = self.n_tensor // 2
        near = self.spread(jnp.stack(held[:split]), False)
        far = self.spread(jnp.stack(held[split:]), True)
        return near, far


    def reduce_half(self, keep, send, groups, out):
        (other,) = yield [(self.partner, send, 0)]
        shape = (2,) * (self.n_bits - 1)
        states = []
        for low, high, flip in groups:
            ours, theirs = (
                a.reshape(shape + a.shape[1:])[..., low:high, :] for a in (keep, other)
            )
            states.append([ours, theirs, self.outer_bits(flip), list(range(self.n_bits - 1, 0, -1))])
        for step in range(self.n_bits - 1):
            moves = []
            for state in states:
                ours, theirs, bits, left = state
                axis = left.index(bits[step])
                pick = lambda a, i: lax.index_in_dim(a, i, axis, keepdims=False)
                moves.append((self.partner, add(pick(ours, 1), pick(theirs, 1)), bits[step]))
                state[0] = add(pick(ours, 0), pick(theirs, 0))
                left.remove(bits[step])
            for state, result in zip(states, (yield moves)):
                state[1] = result
        sums = [add(state[0], state[1]) for state in states]
        out.extend(
            jnp.concatenate([g[j] for g in sums], axis=0) for j in range(sums[0].shape[0])
        )

    def sum_and_spread(self, far, near, flip, out):
        total = far[-1]
        for j in range(self.n_tensor - 2, -1, -1):
            (total,) = yield [(self.turn, total, -1)]
            total = add(total, near[j] if j < len(near) else far[j - len(near)])
        places = [0]
        value = total[None]
        for bit in self.outer_bits(flip):
            (other,) = yield [(self.partner, value, bit)]
            value = jnp.concatenate([value, other], axis=0)
            places = places + [place | 1 << bit for place in places]
        (other,) = yield [(self.partner, value, 0)]
        out.extend([value, other, places])

    def rotate(self, value, out):
        out.append(value)
        for _ in range(self.n_tensor - 1):
            (value,) = yield [(self.turn, value, 1)]
            out.append(value)

    def sum_all(self, value, out):
        for bit in range(self.n_bits):
            (other,) = yield [(self.partner, value, bit)]
            value = value + other
        held = [value]
        for _ in range(self.n_tensor - 1):
            (value,) = yield [(self.turn, held[-1], 1)]
            held.append(value)
        held = self.slots(jnp.stack(held))
        total = held[0]
        for j in range(1, self.n_tensor):
            total = total + held[j]
        out.append(total)

    def round_of(self, chains, *tied):
        results = [[move(value, by) for move, value, by in c.moves] for c in chains]
        results, tied = lax.optimization_barrier((results, tied))
        return [c for c, r in zip(chains, results) if c.advance(r)], tied

    def slots(self, canonical):
        at = (self.tensor_at - jnp.arange(self.n_tensor)) % self.n_tensor
        return jnp.take(canonical, at, axis=0)


class Chain:
    def __init__(self, steps):
        self.steps = steps
        self.moves = next(steps)

    def advance(self, results):
        try:
            self.moves = self.steps.send(results)
        except StopIteration:
            return False
        return True


def body(
    tokens_in, norm1_gain, norm1_bias, w_qkv, bias_qv, w_out, bias_out, norm2_gain, norm2_bias,
    w_up, bias_up, w_down, bias_down, cotangent, *, n_dp, n_tensor,
):
    images, seq_len, width = tokens_in.shape
    _, _, heads, head_size = w_qkv.shape
    inner = heads * head_size
    hidden = w_up.shape[1]
    assert images == n_tensor
    rows = -(-seq_len // 128) * 128
    ring = Ring(n_dp, n_tensor)
    at = jnp.stack([ring.dp_at, ring.tensor_at]).astype(jnp.int32)

    w_qkv_t = jnp.transpose(w_qkv, (1, 2, 3, 0)).reshape(3 * inner, width)
    cut = 3 * inner // n_dp
    attn_part = jnp.concatenate(
        [ring.part_of(w_qkv_t), ring.part_of(w_out.reshape(inner, width))], axis=0
    )
    attn_rows = attn_part.shape[0]
    near, far = ring.gather_slots(attn_part)
    mlp_part = jnp.concatenate([ring.part_of(w_up), ring.part_of(w_down)], axis=0)
    mlp_rows = mlp_part.shape[0]
    wmlp = lax.all_gather(mlp_part, ("dp", "tensor"), axis=0)
    wmlp = wmlp.reshape(n_dp, n_tensor, mlp_rows, width)

    def own_rows(stack):
        image = lax.dynamic_index_in_dim(stack, ring.tensor_at, 0, keepdims=False)
        return jnp.pad(image, ((0, rows - seq_len), (0, 0)))

    x = own_rows(tokens_in)
    c = own_rows(cotangent)
    biases = jnp.concatenate([bias_qv.reshape(2 * inner), bias_up])
    biases = jnp.stack(ring.round_tensor(biases.reshape(-1, 128))).reshape(n_tensor, -1)
    bqkv = jnp.concatenate(
        [biases[:, :inner], jnp.zeros((n_tensor, inner), F32), biases[:, inner : 2 * inner]], axis=1
    )[:, None]
    bup = biases[:, None, 2 * inner :]
    vec = lambda v: v.reshape(1, width)

    row_block = whole((rows, width))
    vec_block = whole((1, width))
    act = lambda dt: jax.ShapeDtypeStruct((rows, width), dt)
    col_block = lambda n: pl.BlockSpec((rows, n), lambda g, *_: (0, g))
    slot_row = pl.BlockSpec((1, 1, 3 * inner), lambda g, *_: (g, 0, 0))
    split = n_tensor // 2
    near_block = pl.BlockSpec(
        (1, attn_rows, width), lambda g, *_: (jnp.minimum(g, split - 1), 0, 0)
    )
    far_block = pl.BlockSpec(
        (1, attn_rows, width), lambda g, *_: (jnp.maximum(g - split, 0), 0, 0)
    )
    piece_blocks = [near_block] * n_dp + [far_block] * n_dp
    weight_scratch = [
        pltpu.VMEM((n_dp, cut, width), BF16),
        pltpu.VMEM((n_dp, attn_rows - cut, width), BF16),
    ]
    u1, qkv, o, hidden1, u2 = call(
        functools.partial(fwd_kernel, n_dp, split, heads, head_size, seq_len),
        (n_tensor,),
        piece_blocks
        + [row_block, vec_block, vec_block, slot_row, vec_block, vec_block, vec_block],
        [row_block, col_block(3 * inner), col_block(inner), row_block, row_block],
        [
            act(BF16), jax.ShapeDtypeStruct((rows, n_tensor * 3 * inner), BF16),
            jax.ShapeDtypeStruct((rows, n_tensor * inner), BF16), act(F32), act(BF16),
        ],
        [pltpu.VMEM((rows, width), F32)] + weight_scratch,
        "attention_forward",
        1,
    )(
        at, *near, *far, x, vec(norm1_gain), vec(norm1_bias), bqkv, vec(bias_out),
        vec(norm2_gain), vec(norm2_bias),
    )

    parts = 2
    image_block = whole((seq_len, width))
    image = jax.ShapeDtypeStruct((seq_len, width), BF16)
    row_scratch = pltpu.VMEM((rows, width), F32)

    slot = lambda g, at: lax.rem(at[1] - g + n_tensor, n_tensor)

    def mlp_blocks(base):
        up = pl.BlockSpec(
            (n_dp, 1, width // n_dp, hidden // parts),
            lambda g, p, at: (0, slot(g + base, at), 0, p),
        )
        dn = pl.BlockSpec(
            (n_dp // parts, 1, hidden // n_dp, width),
            lambda g, p, at: (p, slot(g + base, at), 1, 0),
        )
        pre = pl.BlockSpec((rows, hidden // parts), lambda g, p, at: (0, (g + base) * parts + p))
        return up, pre, dn

    up_block, pre_block, dn_block = mlp_blocks(0)
    pre, block_own = call(
        functools.partial(mlp_fwd_kernel, parts),
        (n_tensor, parts),
        [
            row_block, up_block, pl.BlockSpec((1, 1, hidden // parts), lambda g, p, at: (g, 0, p)),
            dn_block, row_block, vec_block,
        ],
        [pre_block, image_block],
        [jax.ShapeDtypeStruct((rows, n_tensor * hidden), F32), image],
        [row_scratch],
        "mlp_forward",
        1,
    )(at, u2, wmlp, bup, wmlp, hidden1, vec(bias_down))

    def mlp_back(base, last, grad_out, extra):
        up_block, pre_block, dn_block = mlp_blocks(base)
        grad_block = pl.BlockSpec((n_dp // 2, 1, mlp_rows, width), lambda g, p, at: (0, g, 0, 0))
        grad_shape = jax.ShapeDtypeStruct((n_dp // 2, split, mlp_rows, width), BF16)
        outs = [
            grad_block, grad_block,
            pl.BlockSpec((1, 1, hidden // parts), lambda g, p, at: (g, 0, p)), row_block,
        ]
        shapes = [
            grad_shape, grad_shape, jax.ShapeDtypeStruct((split, 1, hidden), F32), act(F32),
        ]
        scratch = [pltpu.VMEM((n_dp, mlp_rows, width), BF16)]
        extra_blocks = []
        if last:
            outs += [whole((4, width))]
            shapes += [jax.ShapeDtypeStruct((4, width), F32)]
            scratch += [row_scratch]
            extra_blocks = [row_block, vec_block, row_block]
        return call(
            functools.partial(mlp_kernel, parts, last),
            (split, parts),
            [row_block, row_block, up_block, pre_block, dn_block] + extra_blocks,
            outs,
            shapes,
            scratch,
            "mlp_back_near" if last else "mlp_back_far",
            1,
        )(at, u2, grad_out, wmlp, pre, wmlp, *extra)

    def attention_back(base, last, pieces, grad_hidden1, extra):
        slot_block = pl.BlockSpec((1, attn_rows, width), lambda g, *_: (g, 0, 0))
        cols = lambda n: pl.BlockSpec((rows, n), lambda g, *_: (0, g + base))
        grad_block = pl.BlockSpec((n_dp // 2, 1, attn_rows, width), lambda g, *_: (0, g, 0, 0))
        grad_shape = jax.ShapeDtypeStruct((n_dp // 2, split, attn_rows, width), BF16)
        outs = [grad_block, grad_block, slot_row]
        shapes = [grad_shape, grad_shape, jax.ShapeDtypeStruct((split, 1, 3 * inner), F32)]
        scratch = [
            pltpu.VMEM((rows, width), BF16), pltpu.VMEM((rows, 3 * inner), F32),
        ] + weight_scratch
        if last:
            outs += [image_block, whole((2, width))]
            shapes += [image, jax.ShapeDtypeStruct((2, width), F32)]
            scratch += [row_scratch]
            extra_blocks = [row_block, vec_block, row_block]
        else:
            outs += [row_block]
            shapes += [act(F32)]
            extra_blocks = []
        return call(
            functools.partial(bwd_kernel, n_dp, last, heads, head_size, seq_len),
            (split,),
            [slot_block] * n_dp
            + [row_block, cols(3 * inner), cols(inner), row_block]
            + extra_blocks,
            outs,
            shapes,
            scratch,
            "attention_back_near" if last else "attention_back_far",
            1,
        )(at, *pieces, u1, qkv, o, grad_hidden1, *extra)

    up_rows = width // n_dp
    groups = ((0, up_rows, False), (up_rows, mlp_rows, True))
    third = -(-width // 384) * 128
    spans = [(low, min(low + third, width)) for low in range(0, width, third)]
    lists = lambda n: [[] for _ in range(n)]
    block_held, grad_held = lists(len(spans)), lists(len(spans))
    rotations = lambda value, held: [
        Chain(ring.rotate(value[:, low:high], out)) for (low, high), out in zip(spans, held)
    ]

    turns = rotations(block_own, block_held)
    keep, send, g_bup_far, dacc = mlp_back(split, False, c, ())
    moved, (keep, send, dacc) = ring.round_of(turns[:2], keep, send, dacc)
    turns = turns[2:] + moved
    mlp_far, mlp_near, attn_far, attn_near = lists(4)
    far_chain = [Chain(ring.reduce_half(keep, send, groups, mlp_far))]

    keep, send, g_bup_near, dh1, small2 = mlp_back(
        0, True, c, (hidden1, vec(norm2_gain), dacc)
    )
    moved, (keep, send, dh1) = ring.round_of(far_chain + turns[:2], keep, send, dh1)
    far_chain, turns = moved[:1], turns[2:] + moved[1:]
    near_chain = [Chain(ring.reduce_half(keep, send, groups, mlp_near))]

    keep, send, g_bqkv_far, acc = attention_back(split, False, far, dh1, ())
    running, (keep, send, acc) = ring.round_of(far_chain + near_chain + turns, keep, send, acc)
    running += [Chain(ring.reduce_half(keep, send, ((0, attn_rows, False),), attn_far))]

    keep, send, g_bqkv_near, grad_own, small1 = attention_back(
        0, True, near, dh1, (x, vec(norm1_gain), acc)
    )
    running, (keep, send, grad_own, small1) = ring.round_of(running, keep, send, grad_own, small1)
    running += [Chain(ring.reduce_half(keep, send, ((0, attn_rows, True),), attn_near))]

    g_bup = jnp.concatenate([g_bup_near, g_bup_far], axis=0)
    g_bqkv = jnp.concatenate([g_bqkv_near, g_bqkv_far], axis=0)[:, 0]
    slot_part = ring.slots(
        jnp.concatenate([g_bup[:, 0], g_bqkv[:, :inner], g_bqkv[:, 2 * inner :]], axis=1)
    )
    packed = jnp.concatenate([small1.reshape(-1), small2.reshape(-1), slot_part.reshape(-1)])
    packed_out, mlp_out, attn_out = lists(3)
    running += [Chain(ring.sum_all(packed.reshape(-1, 128), packed_out))]
    waiting = rotations(grad_own, grad_held)
    mlp_started = attn_started = False
    while running or waiting:
        if len(mlp_far) == split and not mlp_started:
            running += [Chain(ring.sum_and_spread(mlp_far, mlp_near, False, mlp_out))]
            mlp_started = True
        if len(attn_far) == split and not attn_started:
            running += [Chain(ring.sum_and_spread(attn_far, attn_near, True, attn_out))]
            attn_started = True
        if waiting and not any(chain in running for chain in turns):
            turns = [waiting.pop(0)]
            running += turns
        running, _ = ring.round_of(running)

    def ordered(held, first_rows, name):
        mine, other, places = held
        n_rows = mine.shape[1]
        out_shapes = [(n_dp, first_rows, width), (n_dp, n_rows - first_rows, width)]
        first, second = call(
            functools.partial(order_kernel, places),
            (1,),
            [whole(mine.shape)] * 2,
            [whole(shape) for shape in out_shapes],
            [jax.ShapeDtypeStruct(shape, F32) for shape in out_shapes],
            [],
            name,
            1,
        )(at, mine, other)
        return first.reshape(-1, width), second.reshape(-1, width)

    def image_order(held, dtype, name):
        shape = (seq_len, n_tensor, width)
        flat = [value for values in held for value in values]
        out = call(
            functools.partial(images_kernel, spans),
            (1,),
            [whole(value.shape) for value in flat],
            whole(shape),
            jax.ShapeDtypeStruct(shape, dtype),
            [],
            name,
            1,
        )(at, *flat)
        return jnp.transpose(out, (1, 0, 2))

    grad_input = image_order(grad_held, F32, "order_grad_input")
    block_out = image_order(block_held, BF16, "order_block_out")
    grad_w_up, grad_w_down = ordered(mlp_out, up_rows, "order_mlp")
    grad_w_qkv, grad_w_out = ordered(attn_out, cut, "order_attention")
    packed = packed_out[0].reshape(-1)
    grad_w_qkv = jnp.transpose(grad_w_qkv.reshape(3, heads, head_size, width), (3, 0, 1, 2))
    grad_w_out = grad_w_out.reshape(heads, head_size, width)

    vectors = packed[: 6 * width].reshape(6, width)
    mine = lax.dynamic_index_in_dim(
        packed[6 * width :].reshape(n_tensor, -1), ring.tensor_at, 0, keepdims=False
    )
    return (
        block_out,
        grad_input,
        vectors[0],
        vectors[1],
        grad_w_qkv,
        mine[hidden:].reshape(2, heads, head_size),
        grad_w_out,
        vectors[5],
        vectors[3],
        vectors[4],
        grad_w_up,
        mine[:hidden],
        grad_w_down,
        vectors[2],
    )


def solution(mesh):
    placed = (
        P("dp", None, None),
        P(),
        P(),
        P(None, None, "tensor", None),
        P(None, "tensor", None),
        P("tensor", None, None),
        P(),
        P(),
        P(),
        P(None, "tensor"),
        P("tensor"),
        P("tensor", None),
        P(),
        P("dp", None, None),
    )
    return jax.shard_map(
        functools.partial(body, n_dp=mesh.shape["dp"], n_tensor=mesh.shape["tensor"]),
        mesh=mesh,
        in_specs=placed,
        out_specs=(
            P("dp", None, None),
            P("dp", None, None),
            P(),
            P(),
            P(None, None, "tensor", None),
            P(None, "tensor", None),
            P("tensor", None, None),
            P(),
            P(),
            P(),
            P(None, "tensor"),
            P("tensor"),
            P("tensor", None),
            P(),
        ),
        check_vma=False,
    )
```

```python
import functools

import jax
import jax.numpy as jnp
from jax import lax
from jax.experimental import pallas as pl
from jax.experimental.pallas import tpu as pltpu
from jax.sharding import PartitionSpec as P

F32 = jnp.float32
BF16 = jnp.bfloat16
EPS = 1e-06
INV_ROOT2 = 0.7071067811865476
INV_ROOT_2PI = 0.3989422804014327
LOG2E = 1.4426950408889634
VMEM_BYTES = 60 * 1024 * 1024


def mm(a, b):
    return lax.dot_general(a, b, (((1,), (0,)), ((), ())), preferred_element_type=F32)


def mm_nt(a, b):
    return lax.dot_general(a, b, (((1,), (1,)), ((), ())), preferred_element_type=F32)


def mm_tn(a, b):
    return lax.dot_general(a, b, (((0,), (0,)), ((), ())), preferred_element_type=F32)


def whiten(values):
    centred = values - jnp.mean(values, axis=-1, keepdims=True)
    inv_std = lax.rsqrt(jnp.mean(centred * centred, axis=-1, keepdims=True) + EPS)
    return centred * inv_std, inv_std


def norm_back(grad_out, white, inv_std, gain):
    grad_white = grad_out * gain
    inner = (
        grad_white
        - jnp.mean(grad_white, axis=-1, keepdims=True)
        - white * jnp.mean(grad_white * white, axis=-1, keepdims=True)
    )
    return inv_std * inner


def row_sum(values):
    return jnp.sum(values, axis=0, keepdims=True)


def joined(ref):
    block = ref[...]
    return block.reshape(block.shape[0] * block.shape[2], block.shape[3])


def weights_of_slot(at_ref, refs, qkv_ref, out_ref):
    cut = qkv_ref.shape[1]
    for distance, ref in enumerate(refs):
        place = at_ref[0] ^ distance
        qkv_ref[place] = ref[0, :cut]
        out_ref[place] = ref[0, cut:]


def merged(ref):
    block = ref[...]
    return block.reshape(block.shape[0] * block.shape[1], block.shape[2])


def fwd_kernel(n_dp, split, heads, head_size, tokens, at_ref, *refs):
    near, far = refs[:n_dp], refs[n_dp : 2 * n_dp]
    (
        x_ref, g1_ref, b1_ref, bqkv_ref, bout_ref, g2_ref, b2_ref,
        u1_ref, qkv_ref, o_ref, h1_ref, u2_ref, acc_ref, wqkv_ref, wout_ref,
    ) = refs[2 * n_dp :]
    step = pl.program_id(0)

    @pl.when(step < split)
    def _():
        weights_of_slot(at_ref, near, wqkv_ref, wout_ref)

    @pl.when(step >= split)
    def _():
        weights_of_slot(at_ref, far, wqkv_ref, wout_ref)

    @pl.when(step == 0)
    def _():
        white, _ = whiten(x_ref[...].astype(F32))
        u1_ref[...] = (white * g1_ref[...] + b1_ref[...]).astype(BF16)
        acc_ref[...] = jnp.zeros_like(acc_ref)

    qkv = (mm_nt(u1_ref[...], merged(wqkv_ref)) + bqkv_ref[0]).astype(BF16)
    qkv_ref[...] = qkv
    inner = heads * head_size
    rows = qkv.shape[0]
    factor = LOG2E * head_size ** (-0.5)
    real = lax.broadcasted_iota(jnp.int32, (1, rows), 1) < tokens
    outs = []
    for head in range(heads):
        q = qkv[:, head * head_size : (head + 1) * head_size]
        k = qkv[:, inner + head * head_size : inner + (head + 1) * head_size]
        v = qkv[:, 2 * inner + head * head_size : 2 * inner + (head + 1) * head_size]
        scores = jnp.where(real, mm_nt(q, k) * factor, -1e30)
        expos = jnp.exp2(scores - jnp.max(scores, axis=-1, keepdims=True))
        total = jnp.sum(expos, axis=-1, keepdims=True)
        outs.append((mm(expos.astype(BF16), v) / total).astype(BF16))
    o = jnp.concatenate(outs, axis=1)
    o_ref[...] = o
    acc_ref[...] += mm(o, merged(wout_ref))

    @pl.when(step == pl.num_programs(0) - 1)
    def _():
        hidden1 = x_ref[...].astype(F32) + acc_ref[...] + bout_ref[...]
        h1_ref[...] = hidden1
        white, _ = whiten(hidden1)
        u2_ref[...] = (white * g2_ref[...] + b2_ref[...]).astype(BF16)


def mlp_fwd_kernel(
    parts, at_ref, u2_ref, wup_ref, bup_ref, wdn_ref, h1_ref, bdn_ref,
    hid_ref, slope_ref, out_ref, acc_ref,
):
    step = pl.program_id(0) * parts + pl.program_id(1)

    @pl.when(step == 0)
    def _():
        acc_ref[...] = jnp.zeros_like(acc_ref)

    pre = mm(u2_ref[...], joined(wup_ref)) + bup_ref[0]
    half = 0.5 * (1.0 + lax.erf(pre * INV_ROOT2))
    hid = (pre * half).astype(BF16)
    hid_ref[...] = hid
    slope_ref[...] = half + pre * INV_ROOT_2PI * jnp.exp(-0.5 * pre * pre)
    acc_ref[...] += mm(hid, joined(wdn_ref))

    @pl.when(step == pl.num_programs(0) * parts - 1)
    def _():
        out = (h1_ref[...] + acc_ref[...] + bdn_ref[...]).astype(BF16)
        out_ref[...] = out[: out_ref.shape[0]]


def mlp_kernel(
    parts, last, at_ref, u2_ref, c_ref, wup_ref, hid_ref, slope_ref, wdn_ref, *refs
):
    if last:
        (
            h1_ref, g2_ref, dacc_in,
            keep_ref, send_ref, gbup_ref, dh1_ref, small_ref, gw_ref, dacc_ref,
        ) = refs
    else:
        keep_ref, send_ref, gbup_ref, dacc_ref, gw_ref = refs
    part = pl.program_id(1)
    step = pl.program_id(0) * parts + part

    @pl.when(step == 0)
    def _():
        dacc_ref[...] = dacc_in[...] if last else jnp.zeros_like(dacc_ref)

    u2 = u2_ref[...]
    c = c_ref[...]
    hid = hid_ref[...]
    up_rows, dn_rows = wup_ref.shape[2], wdn_ref.shape[2]
    gdn = mm_tn(hid, c).astype(BF16).reshape(wdn_ref.shape[0], dn_rows, c.shape[1])
    dpre = mm_nt(c, joined(wdn_ref)) * slope_ref[...]
    gbup_ref[0] = row_sum(dpre)
    dpre_bf = dpre.astype(BF16)
    gup = mm_tn(u2, dpre_bf).astype(BF16).reshape(wup_ref.shape[0], up_rows, hid.shape[1])
    for at in range(parts):

        @pl.when(part == at)
        def _(at=at):
            span, cols = wdn_ref.shape[0], hid.shape[1]
            gw_ref[at * span : (at + 1) * span, up_rows:, :] = gdn
            gw_ref[:, :up_rows, at * cols : (at + 1) * cols] = gup

    @pl.when(part == parts - 1)
    def _():
        for distance in range(gw_ref.shape[0]):
            ref = send_ref if distance & 1 else keep_ref
            ref[distance >> 1, 0] = gw_ref[at_ref[0] ^ distance]

    dacc_ref[...] += mm_nt(dpre_bf, joined(wup_ref))
    if not last:
        return

    @pl.when(step == pl.num_programs(0) * parts - 1)
    def _():
        white, inv_std = whiten(h1_ref[...])
        du2 = dacc_ref[...]
        cf = c.astype(F32)
        dh1 = cf + norm_back(du2, white, inv_std, g2_ref[...])
        dh1_ref[...] = dh1
        small_ref[...] = jnp.concatenate(
            [row_sum(cf), row_sum(du2 * white), row_sum(du2), row_sum(dh1)], axis=0
        )


def bwd_kernel(n_dp, last, heads, head_size, tokens, at_ref, *refs):
    pieces = refs[:n_dp]
    u1_ref, qkv_ref, o_ref, dh1_ref = refs[n_dp : n_dp + 4]
    if last:
        (
            x_ref, g1_ref, acc_in, keep_ref, send_ref, gbias_ref, gin_ref, small_ref,
            dhb_ref, dqkv_ref, wqkv_ref, wout_ref, acc_ref,
        ) = refs[n_dp + 4 :]
    else:
        (
            keep_ref, send_ref, gbias_ref, acc_ref, dhb_ref, dqkv_ref, wqkv_ref, wout_ref,
        ) = refs[n_dp + 4 :]
    step = pl.program_id(0)
    weights_of_slot(at_ref, pieces, wqkv_ref, wout_ref)

    @pl.when(step == 0)
    def _():
        dhb_ref[...] = dh1_ref[...].astype(BF16)
        acc_ref[...] = acc_in[...] if last else jnp.zeros_like(acc_ref)

    dhb = dhb_ref[...]
    qkv = qkv_ref[...]
    up = mm_nt(dhb, merged(wout_ref)).astype(BF16)
    inner = heads * head_size
    rows = qkv.shape[0]
    scale = head_size ** (-0.5)
    real = lax.broadcasted_iota(jnp.int32, (rows, 1), 0) < tokens
    for head in range(heads):
        q = qkv[:, head * head_size : (head + 1) * head_size]
        k = qkv[:, inner + head * head_size : inner + (head + 1) * head_size]
        v = qkv[:, 2 * inner + head * head_size : 2 * inner + (head + 1) * head_size]
        do = up[:, head * head_size : (head + 1) * head_size]
        scores = jnp.where(real, mm_nt(k, q) * (LOG2E * scale), -1e30)
        expos = jnp.exp2(scores - jnp.max(scores, axis=0, keepdims=True))
        probs = expos * (1.0 / jnp.sum(expos, axis=0, keepdims=True))
        dv = mm(probs.astype(BF16), do)
        dprob = mm_nt(v, do)
        delta = jnp.sum(probs * dprob, axis=0, keepdims=True)
        dscore = (probs * (dprob - delta) * scale).astype(BF16)
        dk = mm(dscore, q)
        dq = mm_tn(dscore, k)
        dqkv_ref[:, head * head_size : (head + 1) * head_size] = dq
        dqkv_ref[:, inner + head * head_size : inner + (head + 1) * head_size] = dk
        dqkv_ref[:, 2 * inner + head * head_size : 2 * inner + (head + 1) * head_size] = dv
    dqkv = dqkv_ref[...]
    gbias_ref[0] = row_sum(dqkv)
    dqkv_bf = dqkv.astype(BF16)
    acc_ref[...] += mm(dqkv_bf, merged(wqkv_ref))
    wqkv_ref[...] = mm_tn(dqkv_bf, u1_ref[...]).astype(BF16).reshape(wqkv_ref.shape)
    wout_ref[...] = mm_tn(o_ref[...], dhb).astype(BF16).reshape(wout_ref.shape)
    cut = wqkv_ref.shape[1]
    for distance in range(n_dp):
        place = at_ref[0] ^ distance
        ref = send_ref if distance & 1 else keep_ref
        ref[distance >> 1, 0, :cut] = wqkv_ref[place]
        ref[distance >> 1, 0, cut:] = wout_ref[place]
    if not last:
        return

    @pl.when(step == pl.num_programs(0) - 1)
    def _():
        white, inv_std = whiten(x_ref[...].astype(F32))
        du1 = acc_ref[...]
        gin = (dh1_ref[...] + norm_back(du1, white, inv_std, g1_ref[...])).astype(BF16)
        gin_ref[...] = gin[: gin_ref.shape[0]]
        small_ref[...] = jnp.concatenate([row_sum(du1 * white), row_sum(du1)], axis=0)


def order_kernel(at_ref, mine_ref, other_ref, first_ref, second_ref):
    cut = first_ref.shape[1]
    for ref, low in ((mine_ref, 0), (other_ref, 1)):
        for index in range(ref.shape[0]):
            place = at_ref[0] ^ (index << 1 | low)
            first_ref[place] = ref[index, :cut].astype(F32)
            second_ref[place] = ref[index, cut:].astype(F32)


def images_kernel(at_ref, *refs):
    out_ref, held = refs[-1], refs[:-1]
    count = len(held)
    for image in range(count):
        back = lax.rem(at_ref[1] - image + count, count)
        chosen = held[0][...]
        for j in range(1, count):
            chosen = jnp.where(back == j, held[j][...], chosen)
        out_ref[:, image, :] = chosen.astype(out_ref.dtype)


def whole(shape):
    return pl.BlockSpec(shape, lambda *_: (0,) * len(shape))


def call(kernel, grid, in_specs, out_specs, out_shape, scratch, name, scalars=0):
    return pl.pallas_call(
        kernel,
        grid_spec=pltpu.PrefetchScalarGridSpec(
            num_scalar_prefetch=scalars,
            grid=grid,
            in_specs=in_specs,
            out_specs=out_specs,
            scratch_shapes=scratch,
        ),
        out_shape=out_shape,
        compiler_params=pltpu.CompilerParams(
            dimension_semantics=("arbitrary",) * len(grid), vmem_limit_bytes=VMEM_BYTES
        ),
        name=name,
    )


def tree_sum(values):
    while len(values) > 1:
        values = [a + b for a, b in zip(values[::2], values[1::2])]
    return values[0]


def add(*values):
    return sum(value.astype(F32) for value in values).astype(BF16)


class Ring:
    def __init__(self, n_dp, n_tensor):
        self.n_dp = n_dp
        self.n_tensor = n_tensor
        self.n_bits = n_dp.bit_length() - 1
        assert 1 << self.n_bits == n_dp
        self.dp_at = lax.axis_index("dp")
        self.tensor_at = lax.axis_index("tensor")

    def turn(self, value, by):
        pairs = [(i, (i + by) % self.n_tensor) for i in range(self.n_tensor)]
        return lax.ppermute(value, "tensor", pairs)

    def exchange(self, value, mask):
        return lax.ppermute(value, "dp", [(i, i ^ mask) for i in range(self.n_dp)])

    def outer_bits(self, flip):
        bits = list(range(1, self.n_bits))
        return bits[::-1] if flip else bits

    def round_tensor(self, value):
        held = [value]
        for _ in range(self.n_tensor - 1):
            held.append(self.turn(held[-1], 1))
        return held

    def spread(self, value, flip):
        pieces = {0: value}
        for bit in self.outer_bits(flip) + [0]:
            for distance in list(pieces):
                pieces[distance | 1 << bit] = self.exchange(pieces[distance], 1 << bit)
        return [pieces[distance] for distance in range(self.n_dp)]

    def part_of(self, shard):
        rows = shard.shape[0] // self.n_dp
        return lax.dynamic_slice_in_dim(shard, self.dp_at * rows, rows, axis=0)

    def gather_slots(self, mine):
        held = self.round_tensor(mine)
        split = self.n_tensor // 2
        near = self.spread(jnp.stack(held[:split]), False)
        far = self.spread(jnp.stack(held[split:]), True)
        return near, far


    def outward(self, pick):
        return [(self.exchange, pick(q), q << 1) for q in range(1, self.n_dp // 2)]

    def reduce_slots(self, keep, send, first):
        (other,) = yield [(self.exchange, send, 1)]
        sums = [add(keep[q], other[q]) for q in range(self.n_dp // 2)]
        came = yield self.outward(lambda q: sums[q])
        total = add(sums[0], *came)
        slots = [total[j] for j in range(total.shape[0])]
        own = [slots[0]] if first == 0 else []
        came = yield [
            (self.turn, value, -(first + j)) for j, value in enumerate(slots) if first + j
        ]
        return own + came

    def reduce_far(self, keep, send, first, out):
        out.extend((yield from self.reduce_slots(keep, send, first)))

    def reduce_near(self, keep, send, far, out):
        near = yield from self.reduce_slots(keep, send, 0)
        total = add(*near, *far)
        came = yield self.outward(lambda q: total)
        mine = jnp.stack([total] + came)
        (other,) = yield [(self.exchange, mine, 1)]
        out.extend([mine, other])

    def rotate(self, value, out):
        out.append(value)
        for _ in range(self.n_tensor - 1):
            (value,) = yield [(self.turn, value, 1)]
            out.append(value)

    def sum_all(self, value, out):
        (other,) = yield [(self.exchange, value, 1)]
        value = value + other
        came = yield self.outward(lambda q: value)
        value = tree_sum([value] + came)
        came = yield [(self.turn, value, j) for j in range(1, self.n_tensor)]
        held = self.slots(jnp.stack([value] + came))
        out.append(tree_sum([held[j] for j in range(self.n_tensor)]))

    def round_of(self, chains, *tied):
        results = [[move(value, by) for move, value, by in c.moves] for c in chains]
        results, tied = lax.optimization_barrier((results, tied))
        return [c for c, r in zip(chains, results) if c.advance(r)], tied

    def slots(self, canonical):
        at = (self.tensor_at - jnp.arange(self.n_tensor)) % self.n_tensor
        return jnp.take(canonical, at, axis=0)


class Chain:
    def __init__(self, steps):
        self.steps = steps
        self.moves = next(steps)

    def advance(self, results):
        try:
            self.moves = self.steps.send(results)
        except StopIteration:
            return False
        return True


def body(
    tokens_in, norm1_gain, norm1_bias, w_qkv, bias_qv, w_out, bias_out, norm2_gain, norm2_bias,
    w_up, bias_up, w_down, bias_down, cotangent, *, n_dp, n_tensor,
):
    images, seq_len, width = tokens_in.shape
    _, _, heads, head_size = w_qkv.shape
    inner = heads * head_size
    hidden = w_up.shape[1]
    assert images == n_tensor
    rows = -(-seq_len // 128) * 128
    ring = Ring(n_dp, n_tensor)
    at = jnp.stack([ring.dp_at, ring.tensor_at]).astype(jnp.int32)

    w_qkv_t = jnp.transpose(w_qkv, (1, 2, 3, 0)).reshape(3 * inner, width)
    cut = 3 * inner // n_dp
    attn_part = jnp.concatenate(
        [ring.part_of(w_qkv_t), ring.part_of(w_out.reshape(inner, width))], axis=0
    )
    attn_rows = attn_part.shape[0]
    near, far = ring.gather_slots(attn_part)
    mlp_part = jnp.concatenate([ring.part_of(w_up), ring.part_of(w_down)], axis=0)
    mlp_rows = mlp_part.shape[0]
    wmlp = lax.all_gather(mlp_part, ("dp", "tensor"), axis=0)
    wmlp = wmlp.reshape(n_dp, n_tensor, mlp_rows, width)

    def own_rows(stack):
        image = lax.dynamic_index_in_dim(stack, ring.tensor_at, 0, keepdims=False)
        return jnp.pad(image, ((0, rows - seq_len), (0, 0)))

    x = own_rows(tokens_in)
    c = own_rows(cotangent)
    biases = jnp.concatenate([bias_qv.reshape(2 * inner), bias_up])
    biases = jnp.stack(ring.round_tensor(biases.reshape(-1, 128))).reshape(n_tensor, -1)
    bqkv = jnp.concatenate(
        [biases[:, :inner], jnp.zeros((n_tensor, inner), F32), biases[:, inner : 2 * inner]], axis=1
    )[:, None]
    bup = biases[:, None, 2 * inner :]
    vec = lambda v: v.reshape(1, width)

    row_block = whole((rows, width))
    vec_block = whole((1, width))
    act = lambda dt: jax.ShapeDtypeStruct((rows, width), dt)
    col_block = lambda n: pl.BlockSpec((rows, n), lambda g, *_: (0, g))
    slot_row = pl.BlockSpec((1, 1, 3 * inner), lambda g, *_: (g, 0, 0))
    split = n_tensor // 2
    near_block = pl.BlockSpec(
        (1, attn_rows, width), lambda g, *_: (jnp.minimum(g, split - 1), 0, 0)
    )
    far_block = pl.BlockSpec(
        (1, attn_rows, width), lambda g, *_: (jnp.maximum(g - split, 0), 0, 0)
    )
    piece_blocks = [near_block] * n_dp + [far_block] * n_dp
    weight_scratch = [
        pltpu.VMEM((n_dp, cut, width), BF16),
        pltpu.VMEM((n_dp, attn_rows - cut, width), BF16),
    ]
    u1, qkv, o, hidden1, u2 = call(
        functools.partial(fwd_kernel, n_dp, split, heads, head_size, seq_len),
        (n_tensor,),
        piece_blocks
        + [row_block, vec_block, vec_block, slot_row, vec_block, vec_block, vec_block],
        [row_block, col_block(3 * inner), col_block(inner), row_block, row_block],
        [
            act(BF16), jax.ShapeDtypeStruct((rows, n_tensor * 3 * inner), BF16),
            jax.ShapeDtypeStruct((rows, n_tensor * inner), BF16), act(F32), act(BF16),
        ],
        [pltpu.VMEM((rows, width), F32)] + weight_scratch,
        "attention_forward",
        1,
    )(
        at, *near, *far, x, vec(norm1_gain), vec(norm1_bias), bqkv, vec(bias_out),
        vec(norm2_gain), vec(norm2_bias),
    )

    parts = 2
    image_block = whole((seq_len, width))
    image = jax.ShapeDtypeStruct((seq_len, width), BF16)
    row_scratch = pltpu.VMEM((rows, width), F32)

    slot = lambda g, at: lax.rem(at[1] - g + n_tensor, n_tensor)

    def mlp_blocks(base):
        up = pl.BlockSpec(
            (n_dp, 1, width // n_dp, hidden // parts),
            lambda g, p, at: (0, slot(g + base, at), 0, p),
        )
        dn = pl.BlockSpec(
            (n_dp // parts, 1, hidden // n_dp, width),
            lambda g, p, at: (p, slot(g + base, at), 1, 0),
        )
        cols = pl.BlockSpec((rows, hidden // parts), lambda g, p, at: (0, (g + base) * parts + p))
        return up, cols, dn

    up_block, hidden_block, dn_block = mlp_blocks(0)
    hid, slope, block_own = call(
        functools.partial(mlp_fwd_kernel, parts),
        (n_tensor, parts),
        [
            row_block, up_block, pl.BlockSpec((1, 1, hidden // parts), lambda g, p, at: (g, 0, p)),
            dn_block, row_block, vec_block,
        ],
        [hidden_block, hidden_block, image_block],
        [
            jax.ShapeDtypeStruct((rows, n_tensor * hidden), BF16),
            jax.ShapeDtypeStruct((rows, n_tensor * hidden), F32), image,
        ],
        [row_scratch],
        "mlp_forward",
        1,
    )(at, u2, wmlp, bup, wmlp, hidden1, vec(bias_down))

    def mlp_back(base, last, grad_out, extra):
        up_block, hidden_block, dn_block = mlp_blocks(base)
        grad_block = pl.BlockSpec((n_dp // 2, 1, mlp_rows, width), lambda g, p, at: (0, g, 0, 0))
        grad_shape = jax.ShapeDtypeStruct((n_dp // 2, split, mlp_rows, width), BF16)
        outs = [
            grad_block, grad_block,
            pl.BlockSpec((1, 1, hidden // parts), lambda g, p, at: (g, 0, p)), row_block,
        ]
        shapes = [
            grad_shape, grad_shape, jax.ShapeDtypeStruct((split, 1, hidden), F32), act(F32),
        ]
        scratch = [pltpu.VMEM((n_dp, mlp_rows, width), BF16)]
        extra_blocks = []
        if last:
            outs += [whole((4, width))]
            shapes += [jax.ShapeDtypeStruct((4, width), F32)]
            scratch += [row_scratch]
            extra_blocks = [row_block, vec_block, row_block]
        return call(
            functools.partial(mlp_kernel, parts, last),
            (split, parts),
            [row_block, row_block, up_block, hidden_block, hidden_block, dn_block] + extra_blocks,
            outs,
            shapes,
            scratch,
            "mlp_back_near" if last else "mlp_back_far",
            1,
        )(at, u2, grad_out, wmlp, hid, slope, wmlp, *extra)

    def attention_back(base, last, pieces, grad_hidden1, extra):
        slot_block = pl.BlockSpec((1, attn_rows, width), lambda g, *_: (g, 0, 0))
        cols = lambda n: pl.BlockSpec((rows, n), lambda g, *_: (0, g + base))
        grad_block = pl.BlockSpec((n_dp // 2, 1, attn_rows, width), lambda g, *_: (0, g, 0, 0))
        grad_shape = jax.ShapeDtypeStruct((n_dp // 2, split, attn_rows, width), BF16)
        outs = [grad_block, grad_block, slot_row]
        shapes = [grad_shape, grad_shape, jax.ShapeDtypeStruct((split, 1, 3 * inner), F32)]
        scratch = [
            pltpu.VMEM((rows, width), BF16), pltpu.VMEM((rows, 3 * inner), F32),
        ] + weight_scratch
        if last:
            outs += [image_block, whole((2, width))]
            shapes += [image, jax.ShapeDtypeStruct((2, width), F32)]
            scratch += [row_scratch]
            extra_blocks = [row_block, vec_block, row_block]
        else:
            outs += [row_block]
            shapes += [act(F32)]
            extra_blocks = []
        return call(
            functools.partial(bwd_kernel, n_dp, last, heads, head_size, seq_len),
            (split,),
            [slot_block] * n_dp
            + [row_block, cols(3 * inner), cols(inner), row_block]
            + extra_blocks,
            outs,
            shapes,
            scratch,
            "attention_back_near" if last else "attention_back_far",
            1,
        )(at, *pieces, u1, qkv, o, grad_hidden1, *extra)

    def ordered(held, first_rows, name):
        n_rows = held[0].shape[1]
        out_shapes = [(n_dp, first_rows, width), (n_dp, n_rows - first_rows, width)]
        return call(
            order_kernel,
            (1,),
            [whole(held[0].shape)] * 2,
            [whole(shape) for shape in out_shapes],
            [jax.ShapeDtypeStruct(shape, F32) for shape in out_shapes],
            [],
            name,
            1,
        )(at, *held)

    def image_order(held, dtype, name):
        shape = (seq_len, n_tensor, width)
        span = width // 4
        return call(
            images_kernel,
            (4,),
            [pl.BlockSpec((seq_len, span), lambda i, *_: (0, i))] * n_tensor,
            pl.BlockSpec((seq_len, n_tensor, span), lambda i, *_: (0, 0, i)),
            jax.ShapeDtypeStruct(shape, dtype),
            [],
            name,
            1,
        )(at, *held)

    block_held, grad_held, mlp_far, attn_far, mlp_out, attn_out, packed_out = ([] for _ in range(7))
    running = [Chain(ring.rotate(block_own, block_held))]
    keep, send, g_bup_far, dacc = mlp_back(split, False, c, ())
    running, (keep, send, dacc) = ring.round_of(running, keep, send, dacc)

    running += [Chain(ring.reduce_far(keep, send, split, mlp_far))]
    keep, send, g_bup_near, dh1, small2 = mlp_back(
        0, True, c, (hidden1, vec(norm2_gain), dacc)
    )
    running, (keep, send, dh1) = ring.round_of(running, keep, send, dh1)

    running += [Chain(ring.reduce_near(keep, send, mlp_far, mlp_out))]
    keep, send, g_bqkv_far, acc = attention_back(split, False, far, dh1, ())
    running, (keep, send, acc) = ring.round_of(running, keep, send, acc)

    running += [Chain(ring.reduce_far(keep, send, split, attn_far))]
    keep, send, g_bqkv_near, grad_own, small1 = attention_back(
        0, True, near, dh1, (x, vec(norm1_gain), acc)
    )
    running, (keep, send, grad_own, small1) = ring.round_of(running, keep, send, grad_own, small1)

    g_bup = jnp.concatenate([g_bup_near, g_bup_far], axis=0)
    g_bqkv = jnp.concatenate([g_bqkv_near, g_bqkv_far], axis=0)[:, 0]
    slot_part = ring.slots(
        jnp.concatenate([g_bup[:, 0], g_bqkv[:, :inner], g_bqkv[:, 2 * inner :]], axis=1)
    )
    packed = jnp.concatenate([small1.reshape(-1), small2.reshape(-1), slot_part.reshape(-1)])
    running = [Chain(ring.rotate(grad_own, grad_held))] + running
    running += [Chain(ring.reduce_near(keep, send, attn_far, attn_out))]
    running += [Chain(ring.sum_all(packed.reshape(-1, 128), packed_out))]
    todo = [
        (block_held, n_tensor, lambda: image_order(block_held, BF16, "order_block_out")),
        (grad_held, n_tensor, lambda: image_order(grad_held, F32, "order_grad_input")),
        (mlp_out, 2, lambda: ordered(mlp_out, width // n_dp, "order_mlp")),
        (attn_out, 2, lambda: ordered(attn_out, cut, "order_attention")),
    ]
    done = [None] * len(todo)
    while running:
        beside = next(
            (i for i, (held, n, _) in enumerate(todo) if done[i] is None and len(held) == n), None
        )
        tied = () if beside is None else (todo[beside][2](),)
        running, tied = ring.round_of(running, *tied)
        if beside is not None:
            done[beside] = tied[0]
    done = [work() if value is None else value for value, (_, _, work) in zip(done, todo)]
    block_out, grad_input = (jnp.transpose(value, (1, 0, 2)) for value in done[:2])
    grad_w_up, grad_w_down = (value.reshape(-1, width) for value in done[2])
    grad_w_qkv, grad_w_out = done[3]
    packed = packed_out[0].reshape(-1)
    grad_w_qkv = jnp.transpose(grad_w_qkv.reshape(3, heads, head_size, width), (3, 0, 1, 2))
    grad_w_out = grad_w_out.reshape(heads, head_size, width)

    vectors = packed[: 6 * width].reshape(6, width)
    mine = lax.dynamic_index_in_dim(
        packed[6 * width :].reshape(n_tensor, -1), ring.tensor_at, 0, keepdims=False
    )
    return (
        block_out,
        grad_input,
        vectors[0],
        vectors[1],
        grad_w_qkv,
        mine[hidden:].reshape(2, heads, head_size),
        grad_w_out,
        vectors[5],
        vectors[3],
        vectors[4],
        grad_w_up,
        mine[:hidden],
        grad_w_down,
        vectors[2],
    )


def solution(mesh):
    placed = (
        P("dp", None, None),
        P(),
        P(),
        P(None, None, "tensor", None),
        P(None, "tensor", None),
        P("tensor", None, None),
        P(),
        P(),
        P(),
        P(None, "tensor"),
        P("tensor"),
        P("tensor", None),
        P(),
        P("dp", None, None),
    )
    return jax.shard_map(
        functools.partial(body, n_dp=mesh.shape["dp"], n_tensor=mesh.shape["tensor"]),
        mesh=mesh,
        in_specs=placed,
        out_specs=(
            P("dp", None, None),
            P("dp", None, None),
            P(),
            P(),
            P(None, None, "tensor", None),
            P(None, "tensor", None),
            P("tensor", None, None),
            P(),
            P(),
            P(),
            P(None, "tensor"),
            P("tensor"),
            P("tensor", None),
            P(),
        ),
        check_vma=False,
    )
```
